256 devices in a mesh: doc: 32 (over z, x), tensor: 8 (over y, core).
Axes of the slice: x: 4, y: 4, z: 8, core: 2. Of those that a mesh axis runs over, the one named last changes fastest.
Arguments:
- hidden: bfloat16 [8192, 14336], P('doc', 'tensor'), may hold values from -33 to 33
- grads: bfloat16 [8192, 4096], P('doc'), may hold values from -61 to 61
- lengths: int32 [64], P('doc'), may hold values from 64 to 128, as said below
Outputs:
- grad_weight: float32 [4096, 14336], P('doc', 'tensor')
- norm_ratio: float32 [64], P('doc')
The draws below stay inside these ranges and needn't reach their ends.
Inputs may be any that keep to these rules, and one draw needn't show every extreme that they name: `lengths`: the valid tokens of a document are the first ones of its slot; some document fills its slot.
All inputs are finite; a program needn't handle non-finite values.
Results may differ from the reference program's by a relative error of at most 0.0003.
Values may be sent and summed in bfloat16 or wider, within the bound.
No kernel may reach another device: no remote copies, remote signals or barrier semaphores. Data moves between devices by JAX's collectives and lax.ppermute only.
A program may use at most 128 MiB of HBM per device.

```python
import math
import jax
import jax.numpy as jnp
from jax import lax

D = 4096
FF = 14336
SLOT = 128
DOC_DEV = 2
DOCS = 64


def draw_hidden(key, part):
    subkeys = jax.random.split(key, 3)
    col_pos = jnp.arange(FF, dtype=jnp.float32) / FF
    col_scale = (0.6 + 1.2 * col_pos) * jnp.exp(jax.random.uniform(subkeys[0], (FF,), jnp.float32, math.log(0.5), math.log(2.0)))
    row_scale = jnp.exp(jax.random.uniform(subkeys[1], (DOCS * SLOT, 1), jnp.float32, math.log(0.5), math.log(2.0)))
    entries = jax.random.normal(subkeys[2], (DOCS * SLOT, FF), jnp.float32)
    entries = jnp.clip(entries, -4.5, 4.5)
    return (entries * row_scale * col_scale[None, :]).astype(jnp.bfloat16)


def draw_grads(key, part):
    subkeys = jax.random.split(key, 4)
    col_scale = jnp.exp(jax.random.uniform(subkeys[0], (D,), jnp.float32, math.log(0.5), math.log(2.0)))
    row_scale = jnp.exp(jax.random.uniform(subkeys[1], (DOCS, SLOT, 1), jnp.float32, math.log(0.5), math.log(2.0)))
    doc_scale = jnp.exp(jax.random.uniform(subkeys[2], (DOCS, 1, 1), jnp.float32, 0.0, math.log(10.0)))
    entries = jax.random.normal(subkeys[3], (DOCS, SLOT, D), jnp.float32)
    entries = jnp.clip(entries, -4.5, 4.5)
    scaled = entries * row_scale * doc_scale * col_scale[None, None, :] / 3.0
    return scaled.reshape(DOCS * SLOT, D).astype(jnp.bfloat16)


def draw_lengths(key, part):
    subkeys = jax.random.split(jax.random.fold_in(key, 17), 2)
    drawn = jax.random.randint(subkeys[0], (DOCS,), SLOT // 2, SLOT + 1, jnp.int32)
    chosen = jax.random.randint(subkeys[1], (), 0, DOCS, jnp.int32)
    return jnp.where(jnp.arange(DOCS, dtype=jnp.int32) == chosen, jnp.int32(SLOT), drawn)


def setup_inputs(seed: int = 0) -> dict:
    seeds = jax.random.split(jax.random.key(seed), 4)
    hidden = draw_hidden(jax.random.fold_in(seeds[3], 71), 0)
    grads = draw_grads(jax.random.fold_in(seeds[3], 71), 0)
    lengths = draw_lengths(jax.random.fold_in(seeds[3], 71), 0)
    return {"hidden": hidden, "grads": grads, "lengths": lengths}


clip_ratio = 2.0
epsilon = 1e-06

def weighted_sum(grad_blocks, hidden_blocks, weights):

    def step_fn(running, inputs):
        grad_one, hidden_one, weight_one = inputs
        product = lax.dot_general(grad_one, hidden_one, (((0,), (0,)), ((), ())), preferred_element_type=jnp.float32)
        return (running + weight_one * product, None)
    start_value = jnp.zeros((grad_blocks.shape[2], hidden_blocks.shape[2]), jnp.float32)
    running, unused = lax.scan(step_fn, start_value, (grad_blocks, hidden_blocks, weights))
    return running

def reference(hidden, grads, lengths):
    doc_count = lengths.shape[0]
    hidden_docs = hidden.reshape(doc_count, SLOT, FF)
    positions = jnp.arange(SLOT, dtype=jnp.int32)
    in_length = positions[None, :] < lengths[:, None]
    grad_docs = jnp.where(in_length[:, :, None], grads.reshape(doc_count, SLOT, D), jnp.zeros((), grads.dtype))

    def doc_square(pair):
        hidden_one, grad_one = pair
        hidden_gram = jnp.dot(hidden_one, hidden_one.T, preferred_element_type=jnp.float32)
        grad_gram = jnp.dot(grad_one, grad_one.T, preferred_element_type=jnp.float32)
        return jnp.sum(hidden_gram * grad_gram)
    squares = lax.map(doc_square, (hidden_docs, grad_docs))
    clip_norm = clip_ratio * math.sqrt(SLOT * FF * D)
    norm_ratio = jnp.sqrt(squares + epsilon) / clip_norm
    weights = jnp.minimum(1.0, 1.0 / norm_ratio) / (clip_ratio * math.sqrt(SLOT * doc_count))
    groups = doc_count // DOC_DEV

    def group_step(running, inputs):
        grad_group, hidden_group, weight_group = inputs
        part_sum = weighted_sum(grad_group, hidden_group, weight_group)
        return (running + part_sum, None)
    start_value = jnp.zeros((D, FF), jnp.float32)
    grad_weight, unused = lax.scan(group_step, start_value, (grad_docs.reshape(groups, DOC_DEV, SLOT, D), hidden_docs.reshape(groups, DOC_DEV, SLOT, FF), weights.reshape(groups, DOC_DEV)))
    return (grad_weight, norm_ratio)
```

```python
import math

import jax
import jax.numpy as jnp
from jax import lax
from jax.experimental import pallas as pl
from jax.experimental.pallas import tpu as pltpu
from jax.sharding import Mesh, PartitionSpec as P

SLOT = 128
CLIP_RATIO = 2.0
EPSILON = 1e-06
NX, NY, NZ = 4, 4, 8
LANES = 128
QUARTER = NZ * LANES // NY
NOTE = 16
PIECE = QUARTER + NOTE
BUNDLE = (NX - 1) * PIECE + NOTE
HALVES = ((4, 3), (3, 4))
LIMIT = 32767.0
MANT = 8192.0
EXTRA = 8
GRANT = 24 * 2**20

SMEM = pl.BlockSpec(memory_space=pltpu.SMEM)
VMEM = pl.BlockSpec(memory_space=pltpu.VMEM)
HBM = pl.BlockSpec(memory_space=pltpu.HBM)
NT = (((1,), (1,)), ((), ()))


def cost(flops, nbytes):
    return pl.CostEstimate(flops=flops, bytes_accessed=nbytes, transcendentals=0)


def near(value):
    return pltpu.with_memory_space_constraint(value, pltpu.VMEM)


def split(value):
    hi = value.astype(jnp.bfloat16)
    rest = value - hi.astype(jnp.float32)
    mid = rest.astype(jnp.bfloat16)
    return hi, mid, (rest - mid.astype(jnp.float32)).astype(jnp.bfloat16)


def prepare_kernel(len_ref, pos_ref, hidden_hbm, grads_hbm, own_ref, s1, s2, s3, note_ref, masked_ref, grads_ref, hidden_ref, sem):
    loads = [
        pltpu.make_async_copy(src.at[pl.ds(d * SLOT, SLOT), :], dst.at[pl.ds(d * SLOT, SLOT), :], sem.at[i, d])
        for d in range(2)
        for i, (src, dst) in enumerate(((grads_hbm, grads_ref), (hidden_hbm, hidden_ref)))
    ]
    for load in loads:
        load.start()
    z, x, y, core = (pos_ref[i] for i in range(4))
    row = lax.broadcasted_iota(jnp.int32, note_ref.shape, 0)
    note = jnp.zeros(note_ref.shape, jnp.float32)
    for d in range(2):
        rows = pl.ds(d * SLOT, SLOT)
        loads[2 * d].wait()
        g = grads_ref[rows, :]
        token = lax.broadcasted_iota(jnp.int32, g.shape, 0)
        m = jnp.where(token < len_ref[d], g.astype(jnp.float32), 0.0).astype(g.dtype)
        masked_ref[rows, :] = m
        loads[2 * d + 1].wait()
        h = hidden_ref[rows, :]
        gram_g = lax.dot_general(m, m, NT, preferred_element_type=jnp.float32)
        gram_h = lax.dot_general(h, h, NT, preferred_element_type=jnp.float32)
        square = jnp.sum(gram_g * gram_h)
        whole = jnp.zeros(note_ref.shape, jnp.float32) + square
        for i, term in enumerate(split(whole)):
            note = jnp.where(row == 3 * d + i, term.astype(jnp.float32), note)
    note = note.astype(note_ref.dtype)
    note_ref[...] = note

    r = lax.broadcasted_iota(jnp.int32, (LANES, LANES), 0)
    c = lax.broadcasted_iota(jnp.int32, (LANES, LANES), 1)
    eye = jnp.where(r == c, 1.0, 0.0).astype(masked_ref.dtype)

    def turned(rows, j, dest):
        block = lax.rem(z + 2 * NZ - 1 - j, NZ) * NX + dest
        piece = masked_ref[rows, pl.ds(pl.multiple_of(block * LANES, LANES), LANES)]
        return lax.dot_general(eye, piece, NT, preferred_element_type=jnp.float32).astype(piece.dtype)

    mine = pl.ds(pl.multiple_of(core * SLOT, SLOT), SLOT)
    for k, send in enumerate((s1, s2, s3), 1):
        dest = lax.rem(x + k, NX)
        for i in range(QUARTER // LANES):
            send[pl.ds(i * LANES, LANES), :] = turned(mine, y * (QUARTER // LANES) + i, dest)
        send[pl.ds(QUARTER, NOTE), :] = note
    for j in range(NZ):
        own_ref[pl.ds(j * LANES, LANES), :] = turned(slice(None), j, x)


def prepare(lengths, pos, hidden, grads):
    piece = pltpu.VMEM((PIECE, LANES), grads.dtype)
    return pl.pallas_call(
        prepare_kernel,
        out_shape=(
            pltpu.VMEM((NZ * LANES, grads.shape[0]), grads.dtype),
            piece,
            piece,
            piece,
            pltpu.VMEM((NOTE, LANES), grads.dtype),
        ),
        in_specs=[SMEM, SMEM, HBM, HBM],
        out_specs=(VMEM,) * 5,
        scratch_shapes=[
            pltpu.VMEM(grads.shape, grads.dtype),
            pltpu.VMEM(grads.shape, grads.dtype),
            pltpu.VMEM(hidden.shape, hidden.dtype),
            pltpu.SemaphoreType.DMA((2, 2)),
        ],
        compiler_params=pltpu.CompilerParams(vmem_limit_bytes=GRANT),
        cost_estimate=cost(4 * 10**8, 5 * 10**6),
    )(
        lengths,
        pos,
        pltpu.with_memory_space_constraint(hidden, pltpu.HBM),
        pltpu.with_memory_space_constraint(grads, pltpu.HBM),
    )


def scale_kernel(clip_norm, factor, pos_ref, own, mine, other, hi_ref, lo_ref, ratio_ref):
    y, core = pos_ref[2], pos_ref[3]

    def square(k, d):
        start = (NX - 1) * PIECE if k == 0 else (k - 1) * PIECE + QUARTER

        def partial(ref, r):
            note = ref[pl.ds(r * BUNDLE + start, NOTE), :].astype(jnp.float32)
            return note[3 * d : 3 * d + 1] + note[3 * d + 1 : 3 * d + 2] + note[3 * d + 2 : 3 * d + 3]

        def of(ref):
            return (partial(ref, 0) + partial(ref, 2)) + (partial(ref, 1) + partial(ref, 3))

        return of(mine) + of(other)

    def ratio(k, d):
        return jnp.sqrt(square(k, d) + EPSILON) / clip_norm

    def weight(r):
        return jnp.minimum(1.0, 1.0 / r) / factor

    def put(rows, cols, value, w):
        scaled = value.astype(jnp.float32) * w
        hi = scaled.astype(hi_ref.dtype)
        hi_ref[rows, cols] = hi
        lo_ref[rows, cols] = (scaled - hi.astype(jnp.float32)).astype(lo_ref.dtype)

    row = lax.broadcasted_iota(jnp.int32, ratio_ref.shape, 0)
    r0, r1 = ratio(0, 0), ratio(0, 1)
    ratio_ref[...] = jnp.where(row == 0, r0, r1)
    for d, r in enumerate((r0, r1)):
        put(slice(None), pl.ds(d * SLOT, SLOT), own[:, pl.ds(d * SLOT, SLOT)], weight(r))
    for k in range(1, NX):
        w = [weight(ratio(k, d)) for d in range(2)]
        for ref, doc in ((mine, core), (other, 1 - core)):
            here = jnp.where(doc == 0, w[0], w[1])
            cols = pl.ds(pl.multiple_of((2 * k + doc) * SLOT, SLOT), SLOT)
            for r in range(NY):
                quarter = lax.rem(y + NY - r, NY)
                rows = pl.ds(pl.multiple_of(quarter * QUARTER, QUARTER), QUARTER)
                put(rows, cols, ref[pl.ds(r * BUNDLE + (k - 1) * PIECE, QUARTER), :], here)


def scale(clip_norm, factor, pos, own, mine, other):
    shape = pltpu.VMEM((own.shape[0], NX * own.shape[1]), own.dtype)
    return pl.pallas_call(
        lambda *refs: scale_kernel(clip_norm, factor, *refs),
        out_shape=(shape, shape, jax.ShapeDtypeStruct((8, LANES), jnp.float32)),
        in_specs=[SMEM] + [VMEM] * 3,
        out_specs=(VMEM,) * 3,
        compiler_params=pltpu.CompilerParams(vmem_limit_bytes=GRANT),
        cost_estimate=cost(4 * 10**6, 6 * 10**6),
    )(pos, near(own), near(mine), near(other))


def decode(code):
    rows = code.shape[0] - EXTRA
    mant = code[rows : rows + 1, :].astype(jnp.int32).astype(jnp.float32)
    expo = code[rows + 1 : rows + 2, :].astype(jnp.int32).astype(jnp.float32)
    step = mant * jnp.exp2(expo) * (1.0 / (MANT * LIMIT))
    return code[:rows, :].astype(jnp.int32).astype(jnp.float32) * step


def encode(total, out_ref):
    rows, width = total.shape
    peak = jnp.max(jnp.abs(total), axis=0, keepdims=True)
    expo = jnp.clip(jnp.floor(jnp.log2(jnp.maximum(peak, 1e-30))), -90.0, 90.0)
    mant = jnp.ceil(peak * jnp.exp2(-expo) * MANT)
    step = mant * jnp.exp2(expo) * (1.0 / (MANT * LIMIT))
    inverse = jnp.where(mant > 0.0, 1.0 / jnp.maximum(step, 1e-37), 0.0)
    q = jnp.clip(jnp.round(total * inverse), -LIMIT, LIMIT)
    row = lax.broadcasted_iota(jnp.int32, (EXTRA, width), 0)
    tail = jnp.where(row == 0, mant, expo)
    out_ref[pl.ds(0, rows), :] = q.astype(jnp.int32).astype(jnp.int16)
    out_ref[pl.ds(rows, EXTRA), :] = tail.astype(jnp.int32).astype(jnp.int16)


def product(rows, hi_ref, lo_ref, h_refs):
    total, token = None, 0
    for h in h_refs:
        size = h.shape[0]
        for g in (hi_ref, lo_ref):
            term = jnp.dot(g[rows, pl.ds(token, size)], h[...], preferred_element_type=jnp.float32)
            total = term if total is None else total + term
        token += size
    return total


def first_kernel(up_j, down_j, hi_ref, lo_ref, *refs):
    *h_refs, up_ref, down_ref = refs
    low = min(up_j, down_j)
    both = product(pl.ds(low * LANES, 2 * LANES), hi_ref, lo_ref, h_refs)
    for j, out_ref in ((up_j, up_ref), (down_j, down_ref)):
        encode(both[(j - low) * LANES : (j - low + 1) * LANES], out_ref)


def rest_kernel(skip, hi_ref, lo_ref, *refs):
    *h_refs, out_ref = refs
    for first, stop in ((0, skip[0]), (skip[1] + 1, NZ)):
        at = first if first == 0 else first - 2
        size = (stop - first) * LANES
        out_ref[pl.ds(at * LANES, size), :] = product(pl.ds(first * LANES, size), hi_ref, lo_ref, h_refs)


def hop_kernel(i, recv_ref, parts_ref, out_ref):
    total = parts_ref[pl.ds(i * LANES, LANES), :] + decode(recv_ref[...])
    encode(total, out_ref)


def last_kernel(i, up_ref, down_ref, parts_ref, out_ref):
    out_ref[...] = parts_ref[pl.ds(i * LANES, LANES), :] + decode(up_ref[...]) + decode(down_ref[...])


def call(kernel, out_shape, flops, *args):
    many = isinstance(out_shape, tuple)
    return pl.pallas_call(
        kernel,
        out_shape=out_shape,
        in_specs=[VMEM] * len(args),
        out_specs=(VMEM,) * len(out_shape) if many else VMEM,
        compiler_params=pltpu.CompilerParams(vmem_limit_bytes=GRANT),
        cost_estimate=cost(flops, 10**6),
    )(*map(near, args))


def shift(value, axis, size, by):
    return lax.ppermute(value, axis, [(i, (i + by) % size) for i in range(size)])


def per_device(hidden, grads, lengths):
    tokens = hidden.shape[0]
    doc_total = lengths.shape[0] * NX * NZ
    ff = hidden.shape[1] * NY * 2
    model_dim = grads.shape[1]
    width = hidden.shape[1] // len(HALVES)
    pos = jnp.stack([lax.axis_index(a) for a in ("z", "x", "y", "core")]).astype(jnp.int32)

    gathered, ready = [], None
    for n in range(len(HALVES)):
        own = lax.slice_in_dim(hidden, n * width, (n + 1) * width, axis=1)
        if ready is not None:
            own, ready = lax.optimization_barrier((own, ready))
        below = shift(own, "x", NX, 1)
        above = shift(own, "x", NX, -1)
        below, above = lax.optimization_barrier((below, above))
        ready = below
        far0 = shift(below[: tokens // 2], "x", NX, 1)
        far1 = shift(above[tokens // 2 :], "x", NX, -1)
        gathered.append((own, below, far0, far1, above))

    own, *sends, note = prepare(lengths, pos, hidden, grads)
    got = [shift(s, "x", NX, k) for k, s in enumerate(sends, 1)]
    bundle = jnp.concatenate(got + [note], axis=0)
    copies = [shift(bundle, "y", NY, r) for r in (1, 2, 3)]
    mine = jnp.concatenate([bundle] + copies, axis=0)
    other = shift(mine, "core", 2, 1)
    clip_norm = CLIP_RATIO * math.sqrt(SLOT * ff * model_dim)
    factor = CLIP_RATIO * math.sqrt(SLOT * doc_total)
    hi, lo, ratio = scale(clip_norm, factor, pos, own, mine, other)

    code = pltpu.VMEM((LANES + EXTRA, width), jnp.int16)
    blocks, parts = [], None
    for (up_hops, down_hops), h in zip(HALVES, gathered):
        up, down = list(range(7 - up_hops, 7)), list(range(down_hops - 1, -1, -1))
        if parts is not None:
            *h, parts = lax.optimization_barrier((*h, parts))
        up_got, down_got = call(
            lambda *r, a=up[0], b=down[0]: first_kernel(a, b, *r), (code, code), 10**9, hi, lo, *h
        )
        skip = (down[0], up[0])
        left = [j for j in range(NZ) if j not in skip]
        parts = call(
            lambda *r, s=skip: rest_kernel(s, *r),
            pltpu.VMEM((len(left) * LANES, width), jnp.float32),
            3 * 10**9,
            hi,
            lo,
            *h,
        )
        up_got, down_got = shift(up_got, "z", NZ, 1), shift(down_got, "z", NZ, -1)
        for n in range(1, max(up_hops, down_hops)):
            for way, order in ((1, up), (-1, down)):
                if n < len(order):
                    i = left.index(order[n])
                    have = up_got if way == 1 else down_got
                    new = call(lambda *r, i=i: hop_kernel(i, *r), code, 10**6, have, parts)
                    new = shift(new, "z", NZ, way)
                    if way == 1:
                        up_got = new
                    else:
                        down_got = new
        i = left.index(NZ - 1)
        blocks.append(
            call(
                lambda *r, i=i: last_kernel(i, *r),
                jax.ShapeDtypeStruct((LANES, width), jnp.float32),
                10**6,
                up_got,
                down_got,
                parts,
            )
        )
    return jnp.concatenate(blocks, axis=1), ratio[:2, 0]


def solution(mesh):
    fine = Mesh(mesh.devices.reshape(NZ, NX, NY, 2), ("z", "x", "y", "core"))
    doc, tensor = ("z", "x"), ("y", "core")
    return jax.shard_map(
        per_device,
        mesh=fine,
        in_specs=(P(doc, tensor), P(doc, None), P(doc)),
        out_specs=(P(doc, tensor), P(doc)),
        check_vma=False,
    )
```

```python
import math

import jax
import jax.numpy as jnp
from jax import lax
from jax.experimental import pallas as pl
from jax.experimental.pallas import tpu as pltpu
from jax.sharding import Mesh, PartitionSpec as P

SLOT = 128
CLIP_RATIO = 2.0
EPSILON = 1e-06
NX, NY, NZ = 4, 4, 8
LANES = 128
QUARTER = NZ * LANES // NY
NOTE = 16
PIECE = QUARTER + NOTE
BUNDLE = (NX - 1) * PIECE + NOTE
HALVES = ((4, 3), (3, 4))
LIMIT = 32767.0
MANT = 8192.0
EXTRA = 8
GRANT = 24 * 2**20

SMEM = pl.BlockSpec(memory_space=pltpu.SMEM)
VMEM = pl.BlockSpec(memory_space=pltpu.VMEM)
HBM = pl.BlockSpec(memory_space=pltpu.HBM)
NT = (((1,), (1,)), ((), ()))


def cost(flops, nbytes):
    return pl.CostEstimate(flops=flops, bytes_accessed=nbytes, transcendentals=0)


def near(value):
    return pltpu.with_memory_space_constraint(value, pltpu.VMEM)


def split(value):
    hi = value.astype(jnp.bfloat16)
    rest = value - hi.astype(jnp.float32)
    mid = rest.astype(jnp.bfloat16)
    return hi, mid, (rest - mid.astype(jnp.float32)).astype(jnp.bfloat16)


def prepare_kernel(pos_ref, hidden_hbm, grads_hbm, own_ref, s1, s2, s3, note_ref, masked_ref, grads_ref, hidden_ref, sem):
    loads = [
        pltpu.make_async_copy(src.at[pl.ds(d * SLOT, SLOT), :], dst.at[pl.ds(d * SLOT, SLOT), :], sem.at[i, d])
        for d in range(2)
        for i, (src, dst) in enumerate(((grads_hbm, grads_ref), (hidden_hbm, hidden_ref)))
    ]
    for load in loads:
        load.start()
    z, x, y, core = (pos_ref[i] for i in range(4))
    row = lax.broadcasted_iota(jnp.int32, note_ref.shape, 0)
    note = jnp.zeros(note_ref.shape, jnp.float32)
    for d in range(2):
        rows = pl.ds(d * SLOT, SLOT)
        loads[2 * d].wait()
        g = grads_ref[rows, :]
        token = lax.broadcasted_iota(jnp.int32, g.shape, 0)
        m = jnp.where(token < pos_ref[4 + d], g.astype(jnp.float32), 0.0).astype(g.dtype)
        masked_ref[rows, :] = m
        loads[2 * d + 1].wait()
        h = hidden_ref[rows, :]
        gram_g = lax.dot_general(m, m, NT, preferred_element_type=jnp.float32)
        gram_h = lax.dot_general(h, h, NT, preferred_element_type=jnp.float32)
        square = jnp.sum(gram_g * gram_h)
        whole = jnp.zeros(note_ref.shape, jnp.float32) + square
        for i, term in enumerate(split(whole)):
            note = jnp.where(row == 3 * d + i, term.astype(jnp.float32), note)
    note = note.astype(note_ref.dtype)
    note_ref[...] = note

    r = lax.broadcasted_iota(jnp.int32, (LANES, LANES), 0)
    c = lax.broadcasted_iota(jnp.int32, (LANES, LANES), 1)
    eye = jnp.where(r == c, 1.0, 0.0).astype(masked_ref.dtype)

    def turned(rows, j, dest):
        block = lax.rem(z + 2 * NZ - 1 - j, NZ) * NX + dest
        piece = masked_ref[rows, pl.ds(pl.multiple_of(block * LANES, LANES), LANES)]
        return lax.dot_general(eye, piece, NT, preferred_element_type=jnp.float32).astype(piece.dtype)

    mine = pl.ds(pl.multiple_of(core * SLOT, SLOT), SLOT)
    for k, send in enumerate((s1, s2, s3), 1):
        dest = lax.rem(x + k, NX)
        for i in range(QUARTER // LANES):
            send[pl.ds(i * LANES, LANES), :] = turned(mine, y * (QUARTER // LANES) + i, dest)
        send[pl.ds(QUARTER, NOTE), :] = note
    for j in range(NZ):
        own_ref[pl.ds(j * LANES, LANES), :] = turned(slice(None), j, x)


def prepare(pos, hidden, grads):
    piece = pltpu.VMEM((PIECE, LANES), grads.dtype)
    return pl.pallas_call(
        prepare_kernel,
        out_shape=(
            pltpu.VMEM((NZ * LANES, grads.shape[0]), grads.dtype),
            piece,
            piece,
            piece,
            pltpu.VMEM((NOTE, LANES), grads.dtype),
        ),
        in_specs=[SMEM, HBM, HBM],
        out_specs=(VMEM,) * 5,
        scratch_shapes=[
            pltpu.VMEM(grads.shape, grads.dtype),
            pltpu.VMEM(grads.shape, grads.dtype),
            pltpu.VMEM(hidden.shape, hidden.dtype),
            pltpu.SemaphoreType.DMA((2, 2)),
        ],
        compiler_params=pltpu.CompilerParams(vmem_limit_bytes=GRANT),
        cost_estimate=cost(4 * 10**8, 5 * 10**6),
    )(
        pos,
        pltpu.with_memory_space_constraint(hidden, pltpu.HBM),
        pltpu.with_memory_space_constraint(grads, pltpu.HBM),
    )


def scale_kernel(clip_norm, factor, pos_ref, own, mine, other, hi_ref, lo_ref, ratio_ref):
    y, core = pos_ref[2], pos_ref[3]

    def square(k, d):
        start = (NX - 1) * PIECE if k == 0 else (k - 1) * PIECE + QUARTER

        def partial(ref, r):
            note = ref[pl.ds(r * BUNDLE + start, NOTE), :].astype(jnp.float32)
            return note[3 * d : 3 * d + 1] + note[3 * d + 1 : 3 * d + 2] + note[3 * d + 2 : 3 * d + 3]

        def of(ref):
            return (partial(ref, 0) + partial(ref, 2)) + (partial(ref, 1) + partial(ref, 3))

        return of(mine) + of(other)

    def ratio(k, d):
        return jnp.sqrt(square(k, d) + EPSILON) / clip_norm

    def weight(r):
        return jnp.minimum(1.0, 1.0 / r) / factor

    def put(rows, cols, value, w):
        scaled = value.astype(jnp.float32) * w
        hi = scaled.astype(hi_ref.dtype)
        hi_ref[rows, cols] = hi
        lo_ref[rows, cols] = (scaled - hi.astype(jnp.float32)).astype(lo_ref.dtype)

    row = lax.broadcasted_iota(jnp.int32, ratio_ref.shape, 0)
    r0, r1 = ratio(0, 0), ratio(0, 1)
    ratio_ref[...] = jnp.where(row == 0, r0, r1)
    for d, r in enumerate((r0, r1)):
        put(slice(None), pl.ds(d * SLOT, SLOT), own[:, pl.ds(d * SLOT, SLOT)], weight(r))
    for k in range(1, NX):
        w = [weight(ratio(k, d)) for d in range(2)]
        for ref, doc in ((mine, core), (other, 1 - core)):
            here = jnp.where(doc == 0, w[0], w[1])
            cols = pl.ds(pl.multiple_of((2 * k + doc) * SLOT, SLOT), SLOT)
            for r in range(NY):
                quarter = lax.rem(y + NY - r, NY)
                rows = pl.ds(pl.multiple_of(quarter * QUARTER, QUARTER), QUARTER)
                put(rows, cols, ref[pl.ds(r * BUNDLE + (k - 1) * PIECE, QUARTER), :], here)


def scale(clip_norm, factor, pos, own, mine, other):
    shape = pltpu.VMEM((own.shape[0], NX * own.shape[1]), own.dtype)
    return pl.pallas_call(
        lambda *refs: scale_kernel(clip_norm, factor, *refs),
        out_shape=(shape, shape, jax.ShapeDtypeStruct((8, LANES), jnp.float32)),
        in_specs=[SMEM] + [VMEM] * 3,
        out_specs=(VMEM,) * 3,
        compiler_params=pltpu.CompilerParams(vmem_limit_bytes=GRANT),
        cost_estimate=cost(4 * 10**6, 6 * 10**6),
    )(pos, near(own), near(mine), near(other))


def decode(code):
    rows = code.shape[0] - EXTRA
    mant = code[rows : rows + 1, :].astype(jnp.int32).astype(jnp.float32)
    expo = code[rows + 1 : rows + 2, :].astype(jnp.int32).astype(jnp.float32)
    step = mant * jnp.exp2(expo) * (1.0 / (MANT * LIMIT))
    return code[:rows, :].astype(jnp.int32).astype(jnp.float32) * step


def encode(total, out_ref):
    rows, width = total.shape
    peak = jnp.max(jnp.abs(total), axis=0, keepdims=True)
    expo = jnp.clip(jnp.floor(jnp.log2(jnp.maximum(peak, 1e-30))), -90.0, 90.0)
    mant = jnp.ceil(peak * jnp.exp2(-expo) * MANT)
    step = mant * jnp.exp2(expo) * (1.0 / (MANT * LIMIT))
    inverse = jnp.where(mant > 0.0, 1.0 / jnp.maximum(step, 1e-37), 0.0)
    q = jnp.clip(jnp.round(total * inverse), -LIMIT, LIMIT)
    row = lax.broadcasted_iota(jnp.int32, (EXTRA, width), 0)
    tail = jnp.where(row == 0, mant, expo)
    out_ref[pl.ds(0, rows), :] = q.astype(jnp.int32).astype(jnp.int16)
    out_ref[pl.ds(rows, EXTRA), :] = tail.astype(jnp.int32).astype(jnp.int16)


def product(rows, hi_ref, lo_ref, h_refs):
    total, token = None, 0
    for h in h_refs:
        size = h.shape[0]
        for g in (hi_ref, lo_ref):
            term = jnp.dot(g[rows, pl.ds(token, size)], h[...], preferred_element_type=jnp.float32)
            total = term if total is None else total + term
        token += size
    return total


def first_kernel(up_j, down_j, hi_ref, lo_ref, *refs):
    *h_refs, up_ref, down_ref = refs
    low = min(up_j, down_j)
    both = product(pl.ds(low * LANES, 2 * LANES), hi_ref, lo_ref, h_refs)
    for j, out_ref in ((up_j, up_ref), (down_j, down_ref)):
        encode(both[(j - low) * LANES : (j - low + 1) * LANES], out_ref)


def rest_kernel(skip, hi_ref, lo_ref, *refs):
    *h_refs, out_ref = refs
    for first, stop in ((0, skip[0]), (skip[1] + 1, NZ)):
        at = first if first == 0 else first - 2
        size = (stop - first) * LANES
        out_ref[pl.ds(at * LANES, size), :] = product(pl.ds(first * LANES, size), hi_ref, lo_ref, h_refs)


def hop_kernel(i, recv_ref, parts_ref, out_ref):
    total = parts_ref[pl.ds(i * LANES, LANES), :] + decode(recv_ref[...])
    encode(total, out_ref)


def last_kernel(places, *refs):
    *in_refs, out_ref = refs
    width = out_ref.shape[1] // len(places)
    for n, i in enumerate(places):
        up_ref, down_ref, parts_ref = in_refs[3 * n : 3 * n + 3]
        total = parts_ref[pl.ds(i * LANES, LANES), :] + decode(up_ref[...]) + decode(down_ref[...])
        out_ref[:, pl.ds(n * width, width)] = total


def call(kernel, out_shape, flops, *args):
    many = isinstance(out_shape, tuple)
    return pl.pallas_call(
        kernel,
        out_shape=out_shape,
        in_specs=[VMEM] * len(args),
        out_specs=(VMEM,) * len(out_shape) if many else VMEM,
        compiler_params=pltpu.CompilerParams(vmem_limit_bytes=GRANT),
        cost_estimate=cost(flops, 10**6),
    )(*map(near, args))


def shift(value, axis, size, by):
    return lax.ppermute(value, axis, [(i, (i + by) % size) for i in range(size)])


def per_device(hidden, grads, lengths):
    tokens = hidden.shape[0]
    doc_total = lengths.shape[0] * NX * NZ
    ff = hidden.shape[1] * NY * 2
    model_dim = grads.shape[1]
    width = hidden.shape[1] // len(HALVES)
    place = [lax.axis_index(a).astype(jnp.int32) for a in ("z", "x", "y", "core")]
    pos = jnp.concatenate([jnp.stack(place), lengths])

    gathered, ready = [], None
    for n in range(len(HALVES)):
        own = lax.slice_in_dim(hidden, n * width, (n + 1) * width, axis=1)
        if ready is not None:
            own, ready = lax.optimization_barrier((own, ready))
        below = shift(own, "x", NX, 1)
        above = shift(own, "x", NX, -1)
        below, above = lax.optimization_barrier((below, above))
        ready = below
        far0 = shift(below[: tokens // 2], "x", NX, 1)
        far1 = shift(above[tokens // 2 :], "x", NX, -1)
        gathered.append((own, below, far0, far1, above))

    own, *sends, note = prepare(pos, hidden, grads)
    got = [shift(s, "x", NX, k) for k, s in enumerate(sends, 1)]
    bundle = jnp.concatenate(got + [note], axis=0)
    copies = [shift(bundle, "y", NY, r) for r in (1, 2, 3)]
    mine = jnp.concatenate([bundle] + copies, axis=0)
    other = shift(mine, "core", 2, 1)
    clip_norm = CLIP_RATIO * math.sqrt(SLOT * ff * model_dim)
    factor = CLIP_RATIO * math.sqrt(SLOT * doc_total)
    hi, lo, ratio = scale(clip_norm, factor, pos, own, mine, other)

    code = pltpu.VMEM((LANES + EXTRA, width), jnp.int16)
    blocks, places = [], []
    for (up_hops, down_hops), h in zip(HALVES, gathered):
        up, down = list(range(7 - up_hops, 7)), list(range(down_hops - 1, -1, -1))
        codes = call(lambda *r, a=up[0], b=down[0]: first_kernel(a, b, *r), (code, code), 10**9, hi, lo, *h)
        codes = list(codes)
        skip = (down[0], up[0])
        left = [j for j in range(NZ) if j not in skip]
        shape = pltpu.VMEM((len(left) * LANES, width), jnp.float32)
        parts = call(lambda *r, s=skip: rest_kernel(s, *r), shape, 3 * 10**9, hi, lo, *h)
        for n in range(max(up_hops, down_hops)):
            for at, (way, order) in enumerate(((1, up), (-1, down))):
                if n < len(order):
                    if n:
                        i = left.index(order[n])
                        codes[at] = call(lambda *r, i=i: hop_kernel(i, *r), code, 10**6, codes[at], parts)
                    codes[at] = shift(codes[at], "z", NZ, way)
        blocks += [*codes, parts]
        places.append(left.index(NZ - 1))
    grad_weight = call(
        lambda *r: last_kernel(places, *r),
        jax.ShapeDtypeStruct((LANES, hidden.shape[1]), jnp.float32),
        10**6,
        *blocks,
    )
    return grad_weight, ratio[:2, 0]


def solution(mesh):
    fine = Mesh(mesh.devices.reshape(NZ, NX, NY, 2), ("z", "x", "y", "core"))
    doc, tensor = ("z", "x"), ("y", "core")
    return jax.shard_map(
        per_device,
        mesh=fine,
        in_specs=(P(doc, tensor), P(doc, None), P(doc)),
        out_specs=(P(doc, tensor), P(doc)),
        check_vma=False,
    )
```

```python
import functools
import math

import jax
import jax.numpy as jnp
from jax import lax
from jax.experimental import pallas as pl
from jax.experimental.pallas import tpu as pltpu
from jax.sharding import Mesh, PartitionSpec as P

SLOT = 128
CLIP_RATIO = 2.0
EPSILON = 1e-06
NX, NY, NZ = 4, 4, 8
LANES = 128
QUARTER = NZ * LANES // NY
NOTE = 16
PIECE = QUARTER + NOTE
BUNDLE = (NX - 1) * PIECE + NOTE
HALVES = ((4, 3, 9), (3, 4, 5))
LATER = ((((0, 2), (4, 6)), ((6, 8),)), (((1, 3), (5, 7)), ((0, 1), (7, 8))))
LIMIT = 32767.0
MANT = 8192.0
EXTRA = 8
GRANT = 24 * 2**20

SMEM = pl.BlockSpec(memory_space=pltpu.SMEM)
VMEM = pl.BlockSpec(memory_space=pltpu.VMEM)
HBM = pl.BlockSpec(memory_space=pltpu.HBM)
NT = (((1,), (1,)), ((), ()))


def cost(flops, nbytes):
    return pl.CostEstimate(flops=flops, bytes_accessed=nbytes, transcendentals=0)


def near(value):
    return pltpu.with_memory_space_constraint(value, pltpu.VMEM)


def split(value):
    hi = value.astype(jnp.bfloat16)
    rest = value - hi.astype(jnp.float32)
    mid = rest.astype(jnp.bfloat16)
    return hi, mid, (rest - mid.astype(jnp.float32)).astype(jnp.bfloat16)


def prepare_kernel(len_hbm, hidden_hbm, grads_hbm, own_ref, s1, s2, s3, note_ref, masked_ref, grads_ref, hidden_ref, len_ref, sem, len_sem):
    lengths = pltpu.make_async_copy(len_hbm, len_ref, len_sem)
    lengths.start()
    loads = [
        pltpu.make_async_copy(src.at[pl.ds(d * SLOT, SLOT), :], dst.at[pl.ds(d * SLOT, SLOT), :], sem.at[i, d])
        for d in range(2)
        for i, (src, dst) in enumerate(((grads_hbm, grads_ref), (hidden_hbm, hidden_ref)))
    ]
    for load in loads:
        load.start()
    z, x, y, core = (lax.axis_index(a) for a in ("z", "x", "y", "core"))
    row = lax.broadcasted_iota(jnp.int32, note_ref.shape, 0)
    note = jnp.zeros(note_ref.shape, jnp.float32)
    for d in range(2):
        rows = pl.ds(d * SLOT, SLOT)
        if d == 0:
            lengths.wait()
        loads[2 * d].wait()
        g = grads_ref[rows, :]
        token = lax.broadcasted_iota(jnp.int32, g.shape, 0)
        m = jnp.where(token < len_ref[d], g.astype(jnp.float32), 0.0).astype(g.dtype)
        masked_ref[rows, :] = m
        loads[2 * d + 1].wait()
        h = hidden_ref[rows, :]
        gram_g = lax.dot_general(m, m, NT, preferred_element_type=jnp.float32)
        gram_h = lax.dot_general(h, h, NT, preferred_element_type=jnp.float32)
        square = jnp.sum(gram_g * gram_h)
        whole = jnp.zeros(note_ref.shape, jnp.float32) + square
        for i, term in enumerate(split(whole)):
            note = jnp.where(row == 3 * d + i, term.astype(jnp.float32), note)
    note = note.astype(note_ref.dtype)
    note_ref[...] = note

    r = lax.broadcasted_iota(jnp.int32, (LANES, LANES), 0)
    c = lax.broadcasted_iota(jnp.int32, (LANES, LANES), 1)
    eye = jnp.where(r == c, 1.0, 0.0).astype(masked_ref.dtype)

    def turned(rows, j, dest):
        block = lax.rem(z + 2 * NZ - 1 - j, NZ) * NX + dest
        piece = masked_ref[rows, pl.ds(pl.multiple_of(block * LANES, LANES), LANES)]
        return lax.dot_general(eye, piece, NT, preferred_element_type=jnp.float32).astype(piece.dtype)

    mine = pl.ds(pl.multiple_of(core * SLOT, SLOT), SLOT)
    for k, send in enumerate((s1, s2, s3), 1):
        dest = lax.rem(x + k, NX)
        for i in range(QUARTER // LANES):
            send[pl.ds(i * LANES, LANES), :] = turned(mine, y * (QUARTER // LANES) + i, dest)
        send[pl.ds(QUARTER, NOTE), :] = note
    for j in range(NZ):
        own_ref[pl.ds(j * LANES, LANES), :] = turned(slice(None), j, x)


def prepare(lengths, hidden, grads):
    piece = pltpu.VMEM((PIECE, LANES), grads.dtype)
    return pl.pallas_call(
        prepare_kernel,
        out_shape=(
            pltpu.VMEM((NZ * LANES, grads.shape[0]), grads.dtype),
            piece,
            piece,
            piece,
            pltpu.VMEM((NOTE, LANES), grads.dtype),
        ),
        in_specs=[HBM, HBM, HBM],
        out_specs=(VMEM,) * 5,
        scratch_shapes=[
            pltpu.VMEM(grads.shape, grads.dtype),
            pltpu.VMEM(grads.shape, grads.dtype),
            pltpu.VMEM(hidden.shape, hidden.dtype),
            pltpu.SMEM(lengths.shape, lengths.dtype),
            pltpu.SemaphoreType.DMA((2, 2)),
            pltpu.SemaphoreType.DMA(()),
        ],
        compiler_params=pltpu.CompilerParams(vmem_limit_bytes=GRANT),
        cost_estimate=cost(4 * 10**8, 5 * 10**6),
    )(
        pltpu.with_memory_space_constraint(lengths, pltpu.HBM),
        pltpu.with_memory_space_constraint(hidden, pltpu.HBM),
        pltpu.with_memory_space_constraint(grads, pltpu.HBM),
    )


def ratio_of(clip_norm, mine, other, k, d):
    start = (NX - 1) * PIECE if k == 0 else (k - 1) * PIECE + QUARTER

    def partial(ref, r):
        note = ref[pl.ds(r * BUNDLE + start, NOTE), :].astype(jnp.float32)
        return note[3 * d : 3 * d + 1] + note[3 * d + 1 : 3 * d + 2] + note[3 * d + 2 : 3 * d + 3]

    def of(ref):
        return (partial(ref, 0) + partial(ref, 2)) + (partial(ref, 1) + partial(ref, 3))

    return jnp.sqrt(of(mine) + of(other) + EPSILON) / clip_norm


def weighted(clip_norm, factor, own, mine, other, quarters, hi_ref, lo_ref):
    y, core = lax.axis_index("y"), lax.axis_index("core")

    def put(rows, cols, value, w):
        scaled = value.astype(jnp.float32) * w
        hi = scaled.astype(hi_ref.dtype)
        hi_ref[rows, cols] = hi
        lo_ref[rows, cols] = (scaled - hi.astype(jnp.float32)).astype(lo_ref.dtype)

    def weight(k, d):
        return jnp.minimum(1.0, 1.0 / ratio_of(clip_norm, mine, other, k, d)) / factor

    w = [[weight(k, d) for d in range(2)] for k in range(NX)]
    for at, q in enumerate(quarters):
        rows = pl.ds(at * QUARTER, QUARTER)
        for d in range(2):
            cols = pl.ds(d * SLOT, SLOT)
            put(rows, cols, own[pl.ds(q * QUARTER, QUARTER), cols], w[0][d])
        r = lax.rem(y + NY - q, NY)
        for k in range(1, NX):
            start = pl.multiple_of(r * BUNDLE + (k - 1) * PIECE, NOTE)
            for ref, doc in ((mine, core), (other, 1 - core)):
                cols = pl.ds(pl.multiple_of((2 * k + doc) * SLOT, SLOT), SLOT)
                put(rows, cols, ref[pl.ds(start, QUARTER), :], jnp.where(doc == 0, w[k][0], w[k][1]))


def scale_kernel(clip_norm, factor, own, mine, other, hi_ref, lo_ref, ratio_ref):
    row = lax.broadcasted_iota(jnp.int32, ratio_ref.shape, 0)
    r0, r1 = (ratio_of(clip_norm, mine, other, 0, d) for d in range(2))
    ratio_ref[...] = jnp.where(row == 0, r0, r1)
    weighted(clip_norm, factor, own, mine, other, range(NY), hi_ref, lo_ref)


def decode(code):
    rows = code.shape[0] - EXTRA
    mant = code[rows : rows + 1, :].astype(jnp.int32).astype(jnp.float32)
    expo = code[rows + 1 : rows + 2, :].astype(jnp.int32).astype(jnp.float32)
    step = mant * jnp.exp2(expo) * (1.0 / (MANT * LIMIT))
    return code[:rows, :].astype(jnp.int32).astype(jnp.float32) * step


def encode(total, out_ref):
    rows, width = total.shape
    peak = jnp.max(jnp.abs(total), axis=0, keepdims=True)
    expo = jnp.clip(jnp.floor(jnp.log2(jnp.maximum(peak, 1e-30))), -90.0, 90.0)
    mant = jnp.ceil(peak * jnp.exp2(-expo) * MANT)
    step = mant * jnp.exp2(expo) * (1.0 / (MANT * LIMIT))
    inverse = jnp.where(mant > 0.0, 1.0 / jnp.maximum(step, 1e-37), 0.0)
    q = jnp.clip(jnp.round(total * inverse), -LIMIT, LIMIT)
    row = lax.broadcasted_iota(jnp.int32, (EXTRA, width), 0)
    tail = jnp.where(row == 0, mant, expo)
    out_ref[pl.ds(0, rows), :] = q.astype(jnp.int32).astype(jnp.int16)
    out_ref[pl.ds(rows, EXTRA), :] = tail.astype(jnp.int32).astype(jnp.int16)


def product(rows, hi_ref, lo_ref, h_refs):
    total, token = None, 0
    for h in h_refs:
        size = h.shape[0]
        for g in (hi_ref, lo_ref):
            term = jnp.dot(g[rows, pl.ds(token, size)], h[...], preferred_element_type=jnp.float32)
            total = term if total is None else total + term
        token += size
    return total


def encode_pair(low, up_j, down_j, hi_ref, lo_ref, rows, h_refs, up_ref, down_ref):
    both = product(rows, hi_ref, lo_ref, h_refs)
    for j, out_ref in ((up_j, up_ref), (down_j, down_ref)):
        encode(both[(j - low) * LANES : (j - low + 1) * LANES], out_ref)


def opening_kernel(clip_norm, factor, own, mine, other, *refs):
    *h_refs, up_ref, down_ref, hi_ref, lo_ref = refs
    weighted(clip_norm, factor, own, mine, other, (1,), hi_ref, lo_ref)
    encode_pair(2, 3, 2, hi_ref, lo_ref, slice(None), h_refs, up_ref, down_ref)


def first_kernel(up_j, down_j, hi_ref, lo_ref, *refs):
    *h_refs, up_ref, down_ref = refs
    low = min(up_j, down_j)
    encode_pair(low, up_j, down_j, hi_ref, lo_ref, pl.ds(low * LANES, 2 * LANES), h_refs, up_ref, down_ref)


def later_kernel(ranges, hi_ref, lo_ref, *refs):
    *h_refs, out_ref = refs
    at = 0
    for first, stop in ranges:
        size = (stop - first) * LANES
        out_ref[pl.ds(at, size), :] = product(pl.ds(first * LANES, size), hi_ref, lo_ref, h_refs)
        at += size


def hop_kernel(i, recv_ref, parts_ref, out_ref):
    total = parts_ref[pl.ds(i * LANES, LANES), :] + decode(recv_ref[...])
    encode(total, out_ref)


def last_kernel(places, *refs):
    *in_refs, out_ref = refs
    at = 0
    for n, i in enumerate(places):
        up_ref, down_ref, parts_ref = in_refs[3 * n : 3 * n + 3]
        total = parts_ref[pl.ds(i * LANES, LANES), :] + decode(up_ref[...]) + decode(down_ref[...])
        out_ref[:, pl.ds(at, total.shape[1])] = total
        at += total.shape[1]


def call(kernel, out_shape, flops, *args, scratch=()):
    many = isinstance(out_shape, tuple)
    return pl.pallas_call(
        kernel,
        out_shape=out_shape,
        in_specs=[VMEM] * len(args),
        out_specs=(VMEM,) * len(out_shape) if many else VMEM,
        scratch_shapes=scratch,
        compiler_params=pltpu.CompilerParams(vmem_limit_bytes=GRANT),
        cost_estimate=cost(flops, 10**6),
    )(*map(near, args))


def shift(value, axis, size, by):
    return lax.ppermute(value, axis, [(i, (i + by) % size) for i in range(size)])


def per_device(hidden, grads, lengths):
    tokens = hidden.shape[0]
    doc_total = lengths.shape[0] * NX * NZ
    ff = hidden.shape[1] * NY * 2
    model_dim = grads.shape[1]
    gathered, ready, at = [], None, 0
    for _, _, units in HALVES:
        own = lax.slice_in_dim(hidden, at, at + units * LANES, axis=1)
        at += units * LANES
        if ready is not None:
            own, ready = lax.optimization_barrier((own, ready))
        below = shift(own, "x", NX, 1)
        above = shift(own, "x", NX, -1)
        below, above = lax.optimization_barrier((below, above))
        ready = below
        far0 = shift(below[: tokens // 2], "x", NX, 1)
        far1 = shift(above[tokens // 2 :], "x", NX, -1)
        gathered.append((own, below, far0, far1, above))

    own, *sends, note = prepare(lengths, hidden, grads)
    got = [shift(s, "x", NX, k) for k, s in enumerate(sends, 1)]
    bundle = jnp.concatenate(got + [note], axis=0)
    copies = [shift(bundle, "y", NY, r) for r in (1, 2, 3)]
    mine = jnp.concatenate([bundle] + copies, axis=0)
    other = shift(mine, "core", 2, 1)
    clip_norm = CLIP_RATIO * math.sqrt(SLOT * ff * model_dim)
    factor = CLIP_RATIO * math.sqrt(SLOT * doc_total)
    packs = (own, mine, other)
    wide = pltpu.VMEM((own.shape[0], NX * tokens), own.dtype)
    narrow = pltpu.VMEM((QUARTER, NX * tokens), own.dtype)
    blocks, places, hi, lo = [], [], None, None
    for half, ((up_hops, down_hops, units), h) in enumerate(zip(HALVES, gathered)):
        up, down = list(range(7 - up_hops, 7)), list(range(down_hops - 1, -1, -1))
        width = units * LANES
        code = pltpu.VMEM((LANES + EXTRA, width), jnp.int16)
        if half == 0:
            kernel = functools.partial(opening_kernel, clip_norm, factor)
            codes = call(kernel, (code, code), 10**9, *packs, *h, scratch=[narrow, narrow])
        else:
            kernel = functools.partial(first_kernel, up[0], down[0])
            codes = call(kernel, (code, code), 10**9, hi, lo, *h)
        codes = list(codes)
        if half == 0:
            kernel = functools.partial(scale_kernel, clip_norm, factor)
            tile = jax.ShapeDtypeStruct((8, LANES), jnp.float32)
            hi, lo, ratio = call(kernel, (wide, wide, tile), 4 * 10**6, *packs)
        parts, home = [], {}
        for n, ranges in enumerate(LATER[half]):
            order = [j for first, stop in ranges for j in range(first, stop)]
            home.update({j: (n, i) for i, j in enumerate(order)})
            shape = pltpu.VMEM((len(order) * LANES, width), jnp.float32)
            parts.append(call(functools.partial(later_kernel, ranges), shape, 10**9, hi, lo, *h))
        for n in range(max(up_hops, down_hops)):
            for at, (way, order) in enumerate(((1, up), (-1, down))):
                if n < len(order):
                    if n:
                        p, i = home[order[n]]
                        kernel = functools.partial(hop_kernel, i)
                        codes[at] = call(kernel, code, 10**6, codes[at], parts[p])
                    codes[at] = shift(codes[at], "z", NZ, way)
        p, i = home[NZ - 1]
        blocks += [*codes, parts[p]]
        places.append(i)
    grad_weight = call(
        functools.partial(last_kernel, tuple(places)),
        jax.ShapeDtypeStruct((LANES, hidden.shape[1]), jnp.float32),
        10**6,
        *blocks,
    )
    return grad_weight, ratio[:2, 0]


def solution(mesh):
    fine = Mesh(mesh.devices.reshape(NZ, NX, NY, 2), ("z", "x", "y", "core"))
    doc, tensor = ("z", "x"), ("y", "core")
    return jax.shard_map(
        per_device,
        mesh=fine,
        in_specs=(P(doc, tensor), P(doc, None), P(doc)),
        out_specs=(P(doc, tensor), P(doc)),
        check_vma=False,
    )
```

```python
import functools
import math

import jax
import jax.numpy as jnp
from jax import lax
from jax.experimental import pallas as pl
from jax.experimental.pallas import tpu as pltpu
from jax.sharding import Mesh, PartitionSpec as P

SLOT = 128
CLIP_RATIO = 2.0
EPSILON = 1e-06
NX, NY, NZ = 4, 4, 8
LANES = 128
QUARTER = NZ * LANES // NY
NOTE = 16
PIECE = QUARTER + NOTE
BUNDLE = (NX - 1) * PIECE + NOTE
HALVES = ((4, 3, 8), (3, 4, 6))
LATER = ((((0, 2), (4, 6)), ((6, 8),)), (((1, 3), (5, 7)), ((0, 1), (7, 8))))
LIMIT = 32767.0
MANT = 8192.0
EXTRA = 8
GROUP = 256
GRANT = 24 * 2**20

SMEM = pl.BlockSpec(memory_space=pltpu.SMEM)
VMEM = pl.BlockSpec(memory_space=pltpu.VMEM)
HBM = pl.BlockSpec(memory_space=pltpu.HBM)
NT = (((1,), (1,)), ((), ()))


def cost(flops, nbytes):
    return pl.CostEstimate(flops=flops, bytes_accessed=nbytes, transcendentals=0)


def near(value):
    return pltpu.with_memory_space_constraint(value, pltpu.VMEM)


def split(value):
    hi = value.astype(jnp.bfloat16)
    rest = value - hi.astype(jnp.float32)
    mid = rest.astype(jnp.bfloat16)
    return hi, mid, (rest - mid.astype(jnp.float32)).astype(jnp.bfloat16)


def turned(masked_ref, rows, j, dest):
    r = lax.broadcasted_iota(jnp.int32, (LANES, LANES), 0)
    c = lax.broadcasted_iota(jnp.int32, (LANES, LANES), 1)
    eye = jnp.where(r == c, 1.0, 0.0).astype(masked_ref.dtype)
    block = lax.rem(lax.axis_index("z") + 2 * NZ - 1 - j, NZ) * NX + dest
    piece = masked_ref[rows, pl.ds(pl.multiple_of(block * LANES, LANES), LANES)]
    return lax.dot_general(eye, piece, NT, preferred_element_type=jnp.float32).astype(piece.dtype)


def turn_kernel(masked_ref, own_ref):
    x = lax.axis_index("x")
    for j in range(NZ):
        own_ref[pl.ds(j * LANES, LANES), :] = turned(masked_ref, slice(None), j, x)


def prepare_kernel(len_hbm, hidden_hbm, grads_hbm, masked_ref, s1, s2, s3, note_ref, grads_ref, hidden_ref, len_ref, sem, len_sem):
    lengths = pltpu.make_async_copy(len_hbm, len_ref, len_sem)
    lengths.start()
    loads = [
        pltpu.make_async_copy(src.at[pl.ds(d * SLOT, SLOT), :], dst.at[pl.ds(d * SLOT, SLOT), :], sem.at[i, d])
        for d in range(2)
        for i, (src, dst) in enumerate(((grads_hbm, grads_ref), (hidden_hbm, hidden_ref)))
    ]
    for load in loads:
        load.start()
    x, y, core = (lax.axis_index(a) for a in ("x", "y", "core"))
    row = lax.broadcasted_iota(jnp.int32, note_ref.shape, 0)
    note = jnp.zeros(note_ref.shape, jnp.float32)
    for d in range(2):
        rows = pl.ds(d * SLOT, SLOT)
        if d == 0:
            lengths.wait()
        loads[2 * d].wait()
        g = grads_ref[rows, :]
        token = lax.broadcasted_iota(jnp.int32, g.shape, 0)
        m = jnp.where(token < len_ref[d], g.astype(jnp.float32), 0.0).astype(g.dtype)
        masked_ref[rows, :] = m
        loads[2 * d + 1].wait()
        h = hidden_ref[rows, :]
        gram_g = lax.dot_general(m, m, NT, preferred_element_type=jnp.float32)
        gram_h = lax.dot_general(h, h, NT, preferred_element_type=jnp.float32)
        square = jnp.sum(gram_g * gram_h)
        whole = jnp.zeros(note_ref.shape, jnp.float32) + square
        for i, term in enumerate(split(whole)):
            note = jnp.where(row == 3 * d + i, term.astype(jnp.float32), note)
    note = note.astype(note_ref.dtype)
    note_ref[...] = note

    mine = pl.ds(pl.multiple_of(core * SLOT, SLOT), SLOT)
    for k, send in enumerate((s1, s2, s3), 1):
        dest = lax.rem(x + k, NX)
        for i in range(QUARTER // LANES):
            send[pl.ds(i * LANES, LANES), :] = turned(masked_ref, mine, y * (QUARTER // LANES) + i, dest)
        send[pl.ds(QUARTER, NOTE), :] = note


def prepare(lengths, hidden, grads):
    piece = pltpu.VMEM((PIECE, LANES), grads.dtype)
    return pl.pallas_call(
        prepare_kernel,
        out_shape=(
            pltpu.VMEM(grads.shape, grads.dtype),
            piece,
            piece,
            piece,
            pltpu.VMEM((NOTE, LANES), grads.dtype),
        ),
        in_specs=[HBM, HBM, HBM],
        out_specs=(VMEM,) * 5,
        scratch_shapes=[
            pltpu.VMEM(grads.shape, grads.dtype),
            pltpu.VMEM(hidden.shape, hidden.dtype),
            pltpu.SMEM(lengths.shape, lengths.dtype),
            pltpu.SemaphoreType.DMA((2, 2)),
            pltpu.SemaphoreType.DMA(()),
        ],
        compiler_params=pltpu.CompilerParams(vmem_limit_bytes=GRANT),
        cost_estimate=cost(4 * 10**8, 5 * 10**6),
    )(
        pltpu.with_memory_space_constraint(lengths, pltpu.HBM),
        pltpu.with_memory_space_constraint(hidden, pltpu.HBM),
        pltpu.with_memory_space_constraint(grads, pltpu.HBM),
    )


def ratio_of(clip_norm, mine, other, k, d):
    start = (NX - 1) * PIECE if k == 0 else (k - 1) * PIECE + QUARTER

    def partial(ref, r):
        note = ref[pl.ds(r * BUNDLE + start, NOTE), :].astype(jnp.float32)
        return note[3 * d : 3 * d + 1] + note[3 * d + 1 : 3 * d + 2] + note[3 * d + 2 : 3 * d + 3]

    def of(ref):
        return (partial(ref, 0) + partial(ref, 2)) + (partial(ref, 1) + partial(ref, 3))

    return jnp.sqrt(of(mine) + of(other) + EPSILON) / clip_norm


def weighted(clip_norm, factor, own, mine, other, quarters, hi_ref, lo_ref):
    y, core = lax.axis_index("y"), lax.axis_index("core")

    def put(rows, cols, value, w):
        scaled = value.astype(jnp.float32) * w
        hi = scaled.astype(hi_ref.dtype)
        hi_ref[rows, cols] = hi
        lo_ref[rows, cols] = (scaled - hi.astype(jnp.float32)).astype(lo_ref.dtype)

    def weight(k, d):
        return jnp.minimum(1.0, 1.0 / ratio_of(clip_norm, mine, other, k, d)) / factor

    w = [[weight(k, d) for d in range(2)] for k in range(NX)]
    for at, q in enumerate(quarters):
        rows = pl.ds(at * QUARTER, QUARTER)
        for d in range(2):
            cols = pl.ds(d * SLOT, SLOT)
            put(rows, cols, own[pl.ds(q * QUARTER, QUARTER), cols], w[0][d])
        r = lax.rem(y + NY - q, NY)
        for k in range(1, NX):
            start = pl.multiple_of(r * BUNDLE + (k - 1) * PIECE, NOTE)
            for ref, doc in ((mine, core), (other, 1 - core)):
                cols = pl.ds(pl.multiple_of((2 * k + doc) * SLOT, SLOT), SLOT)
                put(rows, cols, ref[pl.ds(start, QUARTER), :], jnp.where(doc == 0, w[k][0], w[k][1]))


def scale_kernel(clip_norm, factor, own, mine, other, hi_ref, lo_ref, ratio_ref):
    row = lax.broadcasted_iota(jnp.int32, ratio_ref.shape, 0)
    r0, r1 = (ratio_of(clip_norm, mine, other, 0, d) for d in range(2))
    ratio_ref[...] = jnp.where(row == 0, r0, r1)
    weighted(clip_norm, factor, own, mine, other, range(NY), hi_ref, lo_ref)


def step_of(mant, expo):
    return mant * jnp.exp2(expo) * (1.0 / (MANT * LIMIT))


def decode(code_ref):
    groups = code_ref.shape[0] // LANES
    tail = code_ref[pl.ds(groups * LANES, EXTRA), :].astype(jnp.int32).astype(jnp.float32)
    out = []
    for n in range(groups):
        step = step_of(tail[2 * n : 2 * n + 1], tail[2 * n + 1 : 2 * n + 2])
        out.append(code_ref[pl.ds(n * LANES, LANES), :].astype(jnp.int32).astype(jnp.float32) * step)
    return jnp.concatenate(out, axis=1)


def encode(total, out_ref):
    groups = total.shape[1] // GROUP
    row = lax.broadcasted_iota(jnp.int32, (EXTRA, GROUP), 0)
    tail = jnp.zeros((EXTRA, GROUP), jnp.float32)
    for n in range(groups):
        part = total[:, n * GROUP : (n + 1) * GROUP]
        peak = jnp.max(jnp.abs(part), axis=0, keepdims=True)
        expo = jnp.clip(jnp.floor(jnp.log2(jnp.maximum(peak, 1e-30))), -90.0, 90.0)
        mant = jnp.ceil(peak * jnp.exp2(-expo) * MANT)
        inverse = jnp.where(mant > 0.0, 1.0 / jnp.maximum(step_of(mant, expo), 1e-37), 0.0)
        q = jnp.clip(jnp.round(part * inverse), -LIMIT, LIMIT)
        out_ref[pl.ds(n * LANES, LANES), :] = q.astype(jnp.int32).astype(jnp.int16)
        tail = jnp.where(row == 2 * n, mant, jnp.where(row == 2 * n + 1, expo, tail))
    out_ref[pl.ds(groups * LANES, EXTRA), :] = tail.astype(jnp.int32).astype(jnp.int16)


def product(rows, hi_ref, lo_ref, h_refs):
    total, token = None, 0
    for h in h_refs:
        size = h.shape[0]
        for g in (hi_ref, lo_ref):
            term = jnp.dot(g[rows, pl.ds(token, size)], h[...], preferred_element_type=jnp.float32)
            total = term if total is None else total + term
        token += size
    return total


def encode_pair(low, up_j, down_j, hi_ref, lo_ref, rows, h_refs, up_ref, down_ref):
    both = product(rows, hi_ref, lo_ref, h_refs)
    for j, out_ref in ((up_j, up_ref), (down_j, down_ref)):
        encode(both[(j - low) * LANES : (j - low + 1) * LANES], out_ref)


def opening_kernel(clip_norm, factor, own, mine, other, *refs):
    *h_refs, up_ref, down_ref, hi_ref, lo_ref = refs
    weighted(clip_norm, factor, own, mine, other, (1,), hi_ref, lo_ref)
    encode_pair(2, 3, 2, hi_ref, lo_ref, slice(None), h_refs, up_ref, down_ref)


def first_kernel(up_j, down_j, hi_ref, lo_ref, *refs):
    *h_refs, up_ref, down_ref = refs
    low = min(up_j, down_j)
    encode_pair(low, up_j, down_j, hi_ref, lo_ref, pl.ds(low * LANES, 2 * LANES), h_refs, up_ref, down_ref)


def later_kernel(ranges, hi_ref, lo_ref, *refs):
    *h_refs, out_ref = refs
    at = 0
    for first, stop in ranges:
        size = (stop - first) * LANES
        out_ref[pl.ds(at, size), :] = product(pl.ds(first * LANES, size), hi_ref, lo_ref, h_refs)
        at += size


def hop_kernel(i, recv_ref, parts_ref, out_ref):
    total = parts_ref[pl.ds(i * LANES, LANES), :] + decode(recv_ref)
    encode(total, out_ref)


def last_kernel(places, *refs):
    *in_refs, out_ref = refs
    at = 0
    for n, i in enumerate(places):
        up_ref, down_ref, parts_ref = in_refs[3 * n : 3 * n + 3]
        total = parts_ref[pl.ds(i * LANES, LANES), :] + decode(up_ref) + decode(down_ref)
        out_ref[:, pl.ds(at, total.shape[1])] = total
        at += total.shape[1]


def call(kernel, out_shape, flops, *args, scratch=()):
    many = isinstance(out_shape, tuple)
    return pl.pallas_call(
        kernel,
        out_shape=out_shape,
        in_specs=[VMEM] * len(args),
        out_specs=(VMEM,) * len(out_shape) if many else VMEM,
        scratch_shapes=scratch,
        compiler_params=pltpu.CompilerParams(vmem_limit_bytes=GRANT),
        cost_estimate=cost(flops, 10**6),
    )(*map(near, args))


def shift(value, axis, size, by):
    return lax.ppermute(value, axis, [(i, (i + by) % size) for i in range(size)])


def per_device(hidden, grads, lengths):
    tokens = hidden.shape[0]
    doc_total = lengths.shape[0] * NX * NZ
    ff = hidden.shape[1] * NY * 2
    model_dim = grads.shape[1]
    gathered, ready, at = [], None, 0
    for _, _, units in HALVES:
        own = lax.slice_in_dim(hidden, at, at + units * LANES, axis=1)
        at += units * LANES
        if ready is not None:
            own, ready = lax.optimization_barrier((own, ready))
        below = shift(own, "x", NX, 1)
        above = shift(own, "x", NX, -1)
        below, above = lax.optimization_barrier((below, above))
        ready = below
        far0 = shift(below[: tokens // 2], "x", NX, 1)
        far1 = shift(above[tokens // 2 :], "x", NX, -1)
        gathered.append((own, below, far0, far1, above))

    masked, *sends, note = prepare(lengths, hidden, grads)
    got = [shift(s, "x", NX, k) for k, s in enumerate(sends, 1)]
    bundle = jnp.concatenate(got + [note], axis=0)
    copies = [shift(bundle, "y", NY, r) for r in (1, 2, 3)]
    mine = jnp.concatenate([bundle] + copies, axis=0)
    other = shift(mine, "core", 2, 1)
    own = call(turn_kernel, pltpu.VMEM((NZ * LANES, tokens), grads.dtype), 10**8, masked)
    clip_norm = CLIP_RATIO * math.sqrt(SLOT * ff * model_dim)
    factor = CLIP_RATIO * math.sqrt(SLOT * doc_total)
    packs = (own, mine, other)
    wide = pltpu.VMEM((own.shape[0], NX * tokens), own.dtype)
    narrow = pltpu.VMEM((QUARTER, NX * tokens), own.dtype)
    blocks, places, hi, lo = [], [], None, None
    for half, ((up_hops, down_hops, units), h) in enumerate(zip(HALVES, gathered)):
        up, down = list(range(7 - up_hops, 7)), list(range(down_hops - 1, -1, -1))
        width = units * LANES
        code = pltpu.VMEM((width // GROUP * LANES + EXTRA, GROUP), jnp.int16)
        if half == 0:
            kernel = functools.partial(opening_kernel, clip_norm, factor)
            codes = call(kernel, (code, code), 10**9, *packs, *h, scratch=[narrow, narrow])
        else:
            kernel = functools.partial(first_kernel, up[0], down[0])
            codes = call(kernel, (code, code), 10**9, hi, lo, *h)
        codes = list(codes)
        if half == 0:
            kernel = functools.partial(scale_kernel, clip_norm, factor)
            tile = jax.ShapeDtypeStruct((8, LANES), jnp.float32)
            hi, lo, ratio = call(kernel, (wide, wide, tile), 4 * 10**6, *packs)
        parts, home = [], {}
        for n, ranges in enumerate(LATER[half]):
            order = [j for first, stop in ranges for j in range(first, stop)]
            home.update({j: (n, i) for i, j in enumerate(order)})
            shape = pltpu.VMEM((len(order) * LANES, width), jnp.float32)
            parts.append(call(functools.partial(later_kernel, ranges), shape, 10**9, hi, lo, *h))
        for n in range(max(up_hops, down_hops)):
            for at, (way, order) in enumerate(((1, up), (-1, down))):
                if n < len(order):
                    if n:
                        p, i = home[order[n]]
                        kernel = functools.partial(hop_kernel, i)
                        codes[at] = call(kernel, code, 10**6, codes[at], parts[p])
                    codes[at] = shift(codes[at], "z", NZ, way)
        p, i = home[NZ - 1]
        blocks += [*codes, parts[p]]
        places.append(i)
    grad_weight = call(
        functools.partial(last_kernel, tuple(places)),
        jax.ShapeDtypeStruct((LANES, hidden.shape[1]), jnp.float32),
        10**6,
        *blocks,
    )
    return grad_weight, ratio[:2, 0]


def solution(mesh):
    fine = Mesh(mesh.devices.reshape(NZ, NX, NY, 2), ("z", "x", "y", "core"))
    doc, tensor = ("z", "x"), ("y", "core")
    return jax.shard_map(
        per_device,
        mesh=fine,
        in_specs=(P(doc, tensor), P(doc, None), P(doc)),
        out_specs=(P(doc, tensor), P(doc)),
        check_vma=False,
    )
```

```python
import functools
import math

import jax
import jax.numpy as jnp
from jax import lax
from jax.experimental import pallas as pl
from jax.experimental.pallas import tpu as pltpu
from jax.sharding import Mesh, PartitionSpec as P

SLOT = 128
CLIP_RATIO = 2.0
EPSILON = 1e-06
NX, NY, NZ = 4, 4, 8
LANES = 128
QUARTER = NZ * LANES // NY
NOTE = 16
PIECE = QUARTER + NOTE
BUNDLE = (NX - 1) * PIECE + NOTE
HALVES = ((4, 3, 8), (3, 4, 6))
LATER = ((((0, 2), (4, 6)), ((6, 8),)), (((1, 3), (5, 7)), ((0, 1), (7, 8))))
LIMIT = 32767.0
MANT = 8192.0
EXTRA = 8
GROUP = 256
GRANT = 24 * 2**20

SMEM = pl.BlockSpec(memory_space=pltpu.SMEM)
VMEM = pl.BlockSpec(memory_space=pltpu.VMEM)
HBM = pl.BlockSpec(memory_space=pltpu.HBM)
NT = (((1,), (1,)), ((), ()))


def cost(flops, nbytes):
    return pl.CostEstimate(flops=flops, bytes_accessed=nbytes, transcendentals=0)


def near(value):
    return pltpu.with_memory_space_constraint(value, pltpu.VMEM)


def split(value):
    hi = value.astype(jnp.bfloat16)
    rest = value - hi.astype(jnp.float32)
    mid = rest.astype(jnp.bfloat16)
    return hi, mid, (rest - mid.astype(jnp.float32)).astype(jnp.bfloat16)


def turned(masked_ref, rows, j, dest):
    r = lax.broadcasted_iota(jnp.int32, (LANES, LANES), 0)
    c = lax.broadcasted_iota(jnp.int32, (LANES, LANES), 1)
    eye = jnp.where(r == c, 1.0, 0.0).astype(masked_ref.dtype)
    block = lax.rem(lax.axis_index("z") + 2 * NZ - 1 - j, NZ) * NX + dest
    piece = masked_ref[rows, pl.ds(pl.multiple_of(block * LANES, LANES), LANES)]
    return lax.dot_general(eye, piece, NT, preferred_element_type=jnp.float32).astype(piece.dtype)


def turn_kernel(masked_ref, own_ref):
    x = lax.axis_index("x")
    for j in range(NZ):
        own_ref[pl.ds(j * LANES, LANES), :] = turned(masked_ref, slice(None), j, x)


def prepare_kernel(len_hbm, hidden_hbm, grads_hbm, masked_ref, s1, s2, s3, note_ref, grads_ref, hidden_ref, len_ref, sem, len_sem):
    lengths = pltpu.make_async_copy(len_hbm, len_ref, len_sem)
    lengths.start()
    loads = [
        pltpu.make_async_copy(src.at[pl.ds(d * SLOT, SLOT), :], dst.at[pl.ds(d * SLOT, SLOT), :], sem.at[i, d])
        for d in range(2)
        for i, (src, dst) in enumerate(((grads_hbm, grads_ref), (hidden_hbm, hidden_ref)))
    ]
    for load in loads:
        load.start()
    x, y, core = (lax.axis_index(a) for a in ("x", "y", "core"))
    row = lax.broadcasted_iota(jnp.int32, note_ref.shape, 0)
    note = jnp.zeros(note_ref.shape, jnp.float32)
    for d in range(2):
        rows = pl.ds(d * SLOT, SLOT)
        if d == 0:
            lengths.wait()
        loads[2 * d].wait()
        g = grads_ref[rows, :]
        token = lax.broadcasted_iota(jnp.int32, g.shape, 0)
        m = jnp.where(token < len_ref[d], g.astype(jnp.float32), 0.0).astype(g.dtype)
        masked_ref[rows, :] = m
        loads[2 * d + 1].wait()
        h = hidden_ref[rows, :]
        gram_g = lax.dot_general(m, m, NT, preferred_element_type=jnp.float32)
        gram_h = lax.dot_general(h, h, NT, preferred_element_type=jnp.float32)
        square = jnp.sum(gram_g * gram_h)
        whole = jnp.zeros(note_ref.shape, jnp.float32) + square
        for i, term in enumerate(split(whole)):
            note = jnp.where(row == 3 * d + i, term.astype(jnp.float32), note)
    note = note.astype(note_ref.dtype)
    note_ref[...] = note

    mine = pl.ds(pl.multiple_of(core * SLOT, SLOT), SLOT)
    for k, send in enumerate((s1, s2, s3), 1):
        dest = lax.rem(x + k, NX)
        for i in range(QUARTER // LANES):
            send[pl.ds(i * LANES, LANES), :] = turned(masked_ref, mine, y * (QUARTER // LANES) + i, dest)
        send[pl.ds(QUARTER, NOTE), :] = note


def prepare(lengths, hidden, grads):
    piece = pltpu.VMEM((PIECE, LANES), grads.dtype)
    return pl.pallas_call(
        prepare_kernel,
        out_shape=(
            pltpu.VMEM(grads.shape, grads.dtype),
            piece,
            piece,
            piece,
            pltpu.VMEM((NOTE, LANES), grads.dtype),
        ),
        in_specs=[HBM, HBM, HBM],
        out_specs=(VMEM,) * 5,
        scratch_shapes=[
            pltpu.VMEM(grads.shape, grads.dtype),
            pltpu.VMEM(hidden.shape, hidden.dtype),
            pltpu.SMEM(lengths.shape, lengths.dtype),
            pltpu.SemaphoreType.DMA((2, 2)),
            pltpu.SemaphoreType.DMA(()),
        ],
        compiler_params=pltpu.CompilerParams(vmem_limit_bytes=GRANT),
        cost_estimate=cost(4 * 10**8, 5 * 10**6),
    )(
        pltpu.with_memory_space_constraint(lengths, pltpu.HBM),
        pltpu.with_memory_space_constraint(hidden, pltpu.HBM),
        pltpu.with_memory_space_constraint(grads, pltpu.HBM),
    )


def ratio_of(clip_norm, mine, other, k, d):
    start = (NX - 1) * PIECE if k == 0 else (k - 1) * PIECE + QUARTER

    def partial(ref, r):
        note = ref[pl.ds(r * BUNDLE + start, NOTE), :].astype(jnp.float32)
        return note[3 * d : 3 * d + 1] + note[3 * d + 1 : 3 * d + 2] + note[3 * d + 2 : 3 * d + 3]

    def of(ref):
        return (partial(ref, 0) + partial(ref, 2)) + (partial(ref, 1) + partial(ref, 3))

    return jnp.sqrt(of(mine) + of(other) + EPSILON) / clip_norm


def weighted(clip_norm, factor, own, mine, other, quarters, hi_ref, lo_ref):
    y, core = lax.axis_index("y"), lax.axis_index("core")

    def put(rows, cols, value, w):
        scaled = value.astype(jnp.float32) * w
        hi = scaled.astype(hi_ref.dtype)
        hi_ref[rows, cols] = hi
        lo_ref[rows, cols] = (scaled - hi.astype(jnp.float32)).astype(lo_ref.dtype)

    def weight(k, d):
        return jnp.minimum(1.0, 1.0 / ratio_of(clip_norm, mine, other, k, d)) / factor

    w = [[weight(k, d) for d in range(2)] for k in range(NX)]
    for at, q in enumerate(quarters):
        rows = pl.ds(at * QUARTER, QUARTER)
        for d in range(2):
            cols = pl.ds(d * SLOT, SLOT)
            put(rows, cols, own[pl.ds(q * QUARTER, QUARTER), cols], w[0][d])
        r = lax.rem(y + NY - q, NY)
        for k in range(1, NX):
            start = pl.multiple_of(r * BUNDLE + (k - 1) * PIECE, NOTE)
            for ref, doc in ((mine, core), (other, 1 - core)):
                cols = pl.ds(pl.multiple_of((2 * k + doc) * SLOT, SLOT), SLOT)
                put(rows, cols, ref[pl.ds(start, QUARTER), :], jnp.where(doc == 0, w[k][0], w[k][1]))


def scale_kernel(clip_norm, factor, own, mine, other, hi_ref, lo_ref, ratio_ref):
    row = lax.broadcasted_iota(jnp.int32, ratio_ref.shape, 0)
    r0, r1 = (ratio_of(clip_norm, mine, other, 0, d) for d in range(2))
    ratio_ref[...] = jnp.where(row == 0, r0, r1)
    weighted(clip_norm, factor, own, mine, other, range(NY), hi_ref, lo_ref)


def step_of(mant, expo):
    return mant * jnp.exp2(expo) * (1.0 / (MANT * LIMIT))


def decode(code_ref):
    groups = code_ref.shape[0] // LANES
    tail = code_ref[pl.ds(groups * LANES, EXTRA), :].astype(jnp.int32).astype(jnp.float32)
    out = []
    for n in range(groups):
        step = step_of(tail[2 * n : 2 * n + 1], tail[2 * n + 1 : 2 * n + 2])
        out.append(code_ref[pl.ds(n * LANES, LANES), :].astype(jnp.int32).astype(jnp.float32) * step)
    return jnp.concatenate(out, axis=1)


def encode(total, out_ref):
    groups = total.shape[1] // GROUP
    row = lax.broadcasted_iota(jnp.int32, (EXTRA, GROUP), 0)
    tail = jnp.zeros((EXTRA, GROUP), jnp.float32)
    for n in range(groups):
        part = total[:, n * GROUP : (n + 1) * GROUP]
        peak = jnp.max(jnp.abs(part), axis=0, keepdims=True)
        expo = jnp.clip(jnp.floor(jnp.log2(jnp.maximum(peak, 1e-30))), -90.0, 90.0)
        mant = jnp.ceil(peak * jnp.exp2(-expo) * MANT)
        inverse = jnp.where(mant > 0.0, 1.0 / jnp.maximum(step_of(mant, expo), 1e-37), 0.0)
        q = jnp.clip(jnp.round(part * inverse), -LIMIT, LIMIT)
        out_ref[pl.ds(n * LANES, LANES), :] = q.astype(jnp.int32).astype(jnp.int16)
        tail = jnp.where(row == 2 * n, mant, jnp.where(row == 2 * n + 1, expo, tail))
    out_ref[pl.ds(groups * LANES, EXTRA), :] = tail.astype(jnp.int32).astype(jnp.int16)


def product(rows, hi_ref, lo_ref, h_refs):
    total, token = None, 0
    for h in h_refs:
        size = h.shape[0]
        for g in (hi_ref, lo_ref):
            term = jnp.dot(g[rows, pl.ds(token, size)], h[...], preferred_element_type=jnp.float32)
            total = term if total is None else total + term
        token += size
    return total


def encode_pair(low, up_j, down_j, hi_ref, lo_ref, rows, h_refs, up_ref, down_ref):
    both = product(rows, hi_ref, lo_ref, h_refs)
    for j, out_ref in ((up_j, up_ref), (down_j, down_ref)):
        encode(both[(j - low) * LANES : (j - low + 1) * LANES], out_ref)


def opening_kernel(clip_norm, factor, own, mine, other, *refs):
    *h_refs, up_ref, down_ref, hi_ref, lo_ref = refs
    weighted(clip_norm, factor, own, mine, other, (1,), hi_ref, lo_ref)
    encode_pair(2, 3, 2, hi_ref, lo_ref, slice(None), h_refs, up_ref, down_ref)


def first_kernel(up_j, down_j, hi_ref, lo_ref, *refs):
    *h_refs, up_ref, down_ref = refs
    low = min(up_j, down_j)
    encode_pair(low, up_j, down_j, hi_ref, lo_ref, pl.ds(low * LANES, 2 * LANES), h_refs, up_ref, down_ref)


def later_kernel(ranges, hi_ref, lo_ref, *refs):
    *h_refs, out_ref = refs
    at = 0
    for first, stop in ranges:
        size = (stop - first) * LANES
        out_ref[pl.ds(at, size), :] = product(pl.ds(first * LANES, size), hi_ref, lo_ref, h_refs)
        at += size


def hop_kernel(i, recv_ref, parts_ref, out_ref):
    total = parts_ref[pl.ds(i * LANES, LANES), :] + decode(recv_ref)
    encode(total, out_ref)


def last_kernel(i, first, up_ref, down_ref, parts_ref, *refs):
    out_hbm, total_ref, sem = refs[-3:]
    total_ref[...] = parts_ref[pl.ds(i * LANES, LANES), :] + decode(up_ref) + decode(down_ref)
    store = pltpu.make_async_copy(total_ref, out_hbm.at[:, pl.ds(first, total_ref.shape[1])], sem)
    store.start()
    store.wait()


def last(i, first, full, up, down, parts, before):
    width = parts.shape[1]
    args = tuple(map(near, (up, down, parts)))
    aliases = {}
    if before is not None:
        args += (before,)
        aliases = {3: 0}
    return pl.pallas_call(
        functools.partial(last_kernel, i, first),
        out_shape=jax.ShapeDtypeStruct((LANES, full), jnp.float32),
        in_specs=[VMEM] * 3 + [HBM] * (len(args) - 3),
        out_specs=HBM,
        scratch_shapes=[pltpu.VMEM((LANES, width), jnp.float32), pltpu.SemaphoreType.DMA(())],
        input_output_aliases=aliases,
        compiler_params=pltpu.CompilerParams(vmem_limit_bytes=GRANT),
        cost_estimate=cost(10**6, 10**6),
    )(*args)


def call(kernel, out_shape, flops, *args, scratch=()):
    many = isinstance(out_shape, tuple)
    return pl.pallas_call(
        kernel,
        out_shape=out_shape,
        in_specs=[VMEM] * len(args),
        out_specs=(VMEM,) * len(out_shape) if many else VMEM,
        scratch_shapes=scratch,
        compiler_params=pltpu.CompilerParams(vmem_limit_bytes=GRANT),
        cost_estimate=cost(flops, 10**6),
    )(*map(near, args))


def shift(value, axis, size, by):
    return lax.ppermute(value, axis, [(i, (i + by) % size) for i in range(size)])


def per_device(hidden, grads, lengths):
    tokens = hidden.shape[0]
    doc_total = lengths.shape[0] * NX * NZ
    ff = hidden.shape[1] * NY * 2
    model_dim = grads.shape[1]
    gathered, ready, at = [], None, 0
    for _, _, units in HALVES:
        own = lax.slice_in_dim(hidden, at, at + units * LANES, axis=1)
        at += units * LANES
        if ready is not None:
            own, ready = lax.optimization_barrier((own, ready))
        below = shift(own, "x", NX, 1)
        above = shift(own, "x", NX, -1)
        below, above = lax.optimization_barrier((below, above))
        ready = below
        far0 = shift(below[: tokens // 2], "x", NX, 1)
        far1 = shift(above[tokens // 2 :], "x", NX, -1)
        gathered.append((own, below, far0, far1, above))

    masked, *sends, note = prepare(lengths, hidden, grads)
    got = [shift(s, "x", NX, k) for k, s in enumerate(sends, 1)]
    bundle = jnp.concatenate(got + [note], axis=0)
    copies = [shift(bundle, "y", NY, r) for r in (1, 2, 3)]
    mine = jnp.concatenate([bundle] + copies, axis=0)
    other = shift(mine, "core", 2, 1)
    own = call(turn_kernel, pltpu.VMEM((NZ * LANES, tokens), grads.dtype), 10**8, masked)
    clip_norm = CLIP_RATIO * math.sqrt(SLOT * ff * model_dim)
    factor = CLIP_RATIO * math.sqrt(SLOT * doc_total)
    packs = (own, mine, other)
    wide = pltpu.VMEM((own.shape[0], NX * tokens), own.dtype)
    narrow = pltpu.VMEM((QUARTER, NX * tokens), own.dtype)
    grad_weight, first, hi, lo = None, 0, None, None
    for half, ((up_hops, down_hops, units), h) in enumerate(zip(HALVES, gathered)):
        up, down = list(range(7 - up_hops, 7)), list(range(down_hops - 1, -1, -1))
        width = units * LANES
        code = pltpu.VMEM((width // GROUP * LANES + EXTRA, GROUP), jnp.int16)
        if half == 0:
            kernel = functools.partial(opening_kernel, clip_norm, factor)
            codes = call(kernel, (code, code), 10**9, *packs, *h, scratch=[narrow, narrow])
        else:
            kernel = functools.partial(first_kernel, up[0], down[0])
            codes = call(kernel, (code, code), 10**9, hi, lo, *h)
        codes = list(codes)
        if half == 0:
            kernel = functools.partial(scale_kernel, clip_norm, factor)
            tile = jax.ShapeDtypeStruct((8, LANES), jnp.float32)
            hi, lo, ratio = call(kernel, (wide, wide, tile), 4 * 10**6, *packs)
        parts, home = [], {}
        for n, ranges in enumerate(LATER[half]):
            order = [j for start, stop in ranges for j in range(start, stop)]
            home.update({j: (n, i) for i, j in enumerate(order)})
            shape = pltpu.VMEM((len(order) * LANES, width), jnp.float32)
            parts.append(call(functools.partial(later_kernel, ranges), shape, 10**9, hi, lo, *h))
        for n in range(max(up_hops, down_hops)):
            for at, (way, order) in enumerate(((1, up), (-1, down))):
                if n < len(order):
                    if n:
                        p, i = home[order[n]]
                        kernel = functools.partial(hop_kernel, i)
                        codes[at] = call(kernel, code, 10**6, codes[at], parts[p])
                    codes[at] = shift(codes[at], "z", NZ, way)
        p, i = home[NZ - 1]
        grad_weight = last(i, first, hidden.shape[1], *codes, parts[p], grad_weight)
        first += width
    return grad_weight, ratio[:2, 0]


def solution(mesh):
    fine = Mesh(mesh.devices.reshape(NZ, NX, NY, 2), ("z", "x", "y", "core"))
    doc, tensor = ("z", "x"), ("y", "core")
    return jax.shard_map(
        per_device,
        mesh=fine,
        in_specs=(P(doc, tensor), P(doc, None), P(doc)),
        out_specs=(P(doc, tensor), P(doc)),
        check_vma=False,
    )
```

```python
import functools
import math

import jax
import jax.numpy as jnp
from jax import lax
from jax.experimental import pallas as pl
from jax.experimental.pallas import tpu as pltpu
from jax.sharding import Mesh, PartitionSpec as P

SLOT = 128
CLIP_RATIO = 2.0
EPSILON = 1e-06
NX, NY, NZ = 4, 4, 8
LANES = 128
QUARTER = NZ * LANES // NY
NOTE = 16
PIECE = QUARTER + NOTE
BUNDLE = (NX - 1) * PIECE + NOTE
HALVES = ((4, 3, (4, 4)), (3, 4, (6,)))
LATER = ((((0, 2), (4, 6)), ((6, 8),)), (((1, 3), (5, 7)), ((0, 1), (7, 8))))
LIMIT = 32767.0
MANT = 8192.0
EXTRA = 8
GROUP = 256
GRANT = 24 * 2**20

SMEM = pl.BlockSpec(memory_space=pltpu.SMEM)
VMEM = pl.BlockSpec(memory_space=pltpu.VMEM)
HBM = pl.BlockSpec(memory_space=pltpu.HBM)
NT = (((1,), (1,)), ((), ()))


def cost(flops, nbytes):
    return pl.CostEstimate(flops=flops, bytes_accessed=nbytes, transcendentals=0)


def near(value):
    return pltpu.with_memory_space_constraint(value, pltpu.VMEM)


def split(value):
    hi = value.astype(jnp.bfloat16)
    rest = value - hi.astype(jnp.float32)
    mid = rest.astype(jnp.bfloat16)
    return hi, mid, (rest - mid.astype(jnp.float32)).astype(jnp.bfloat16)


def turned(masked_ref, rows, j, dest):
    r = lax.broadcasted_iota(jnp.int32, (LANES, LANES), 0)
    c = lax.broadcasted_iota(jnp.int32, (LANES, LANES), 1)
    eye = jnp.where(r == c, 1.0, 0.0).astype(masked_ref.dtype)
    block = lax.rem(lax.axis_index("z") + 2 * NZ - 1 - j, NZ) * NX + dest
    piece = masked_ref[rows, pl.ds(pl.multiple_of(block * LANES, LANES), LANES)]
    return lax.dot_general(eye, piece, NT, preferred_element_type=jnp.float32).astype(piece.dtype)


def turn_kernel(masked_ref, own_ref):
    x = lax.axis_index("x")
    for j in range(NZ):
        own_ref[pl.ds(j * LANES, LANES), :] = turned(masked_ref, slice(None), j, x)


def prepare_kernel(len_hbm, hidden_hbm, grads_hbm, masked_ref, s1, s2, s3, note_ref, grads_ref, hidden_ref, len_ref, sem, len_sem):
    lengths = pltpu.make_async_copy(len_hbm, len_ref, len_sem)
    lengths.start()
    loads = [
        pltpu.make_async_copy(src.at[pl.ds(d * SLOT, SLOT), :], dst.at[pl.ds(d * SLOT, SLOT), :], sem.at[i, d])
        for d in range(2)
        for i, (src, dst) in enumerate(((grads_hbm, grads_ref), (hidden_hbm, hidden_ref)))
    ]
    for load in loads:
        load.start()
    x, y, core = (lax.axis_index(a) for a in ("x", "y", "core"))
    row = lax.broadcasted_iota(jnp.int32, note_ref.shape, 0)
    note = jnp.zeros(note_ref.shape, jnp.float32)
    for d in range(2):
        rows = pl.ds(d * SLOT, SLOT)
        if d == 0:
            lengths.wait()
        loads[2 * d].wait()
        g = grads_ref[rows, :]
        token = lax.broadcasted_iota(jnp.int32, g.shape, 0)
        m = jnp.where(token < len_ref[d], g.astype(jnp.float32), 0.0).astype(g.dtype)
        masked_ref[rows, :] = m
        loads[2 * d + 1].wait()
        h = hidden_ref[rows, :]
        gram_g = lax.dot_general(m, m, NT, preferred_element_type=jnp.float32)
        gram_h = lax.dot_general(h, h, NT, preferred_element_type=jnp.float32)
        square = jnp.sum(gram_g * gram_h)
        whole = jnp.zeros(note_ref.shape, jnp.float32) + square
        for i, term in enumerate(split(whole)):
            note = jnp.where(row == 3 * d + i, term.astype(jnp.float32), note)
    note = note.astype(note_ref.dtype)
    note_ref[...] = note

    mine = pl.ds(pl.multiple_of(core * SLOT, SLOT), SLOT)
    for k, send in enumerate((s1, s2, s3), 1):
        dest = lax.rem(x + k, NX)
        for i in range(QUARTER // LANES):
            send[pl.ds(i * LANES, LANES), :] = turned(masked_ref, mine, y * (QUARTER // LANES) + i, dest)
        send[pl.ds(QUARTER, NOTE), :] = note


def prepare(lengths, hidden, grads):
    piece = pltpu.VMEM((PIECE, LANES), grads.dtype)
    return pl.pallas_call(
        prepare_kernel,
        out_shape=(
            pltpu.VMEM(grads.shape, grads.dtype),
            piece,
            piece,
            piece,
            pltpu.VMEM((NOTE, LANES), grads.dtype),
        ),
        in_specs=[HBM, HBM, HBM],
        out_specs=(VMEM,) * 5,
        scratch_shapes=[
            pltpu.VMEM(grads.shape, grads.dtype),
            pltpu.VMEM(hidden.shape, hidden.dtype),
            pltpu.SMEM(lengths.shape, lengths.dtype),
            pltpu.SemaphoreType.DMA((2, 2)),
            pltpu.SemaphoreType.DMA(()),
        ],
        compiler_params=pltpu.CompilerParams(vmem_limit_bytes=GRANT),
        cost_estimate=cost(4 * 10**8, 5 * 10**6),
    )(
        pltpu.with_memory_space_constraint(lengths, pltpu.HBM),
        pltpu.with_memory_space_constraint(hidden, pltpu.HBM),
        pltpu.with_memory_space_constraint(grads, pltpu.HBM),
    )


def ratio_of(clip_norm, mine, other, k, d):
    start = (NX - 1) * PIECE if k == 0 else (k - 1) * PIECE + QUARTER

    def partial(ref, r):
        note = ref[pl.ds(r * BUNDLE + start, NOTE), :].astype(jnp.float32)
        return note[3 * d : 3 * d + 1] + note[3 * d + 1 : 3 * d + 2] + note[3 * d + 2 : 3 * d + 3]

    def of(ref):
        return (partial(ref, 0) + partial(ref, 2)) + (partial(ref, 1) + partial(ref, 3))

    return jnp.sqrt(of(mine) + of(other) + EPSILON) / clip_norm


def weighted(clip_norm, factor, own, mine, other, quarters, hi_ref, lo_ref):
    y, core = lax.axis_index("y"), lax.axis_index("core")

    def put(rows, cols, value, w):
        scaled = value.astype(jnp.float32) * w
        hi = scaled.astype(hi_ref.dtype)
        hi_ref[rows, cols] = hi
        lo_ref[rows, cols] = (scaled - hi.astype(jnp.float32)).astype(lo_ref.dtype)

    def weight(k, d):
        return jnp.minimum(1.0, 1.0 / ratio_of(clip_norm, mine, other, k, d)) / factor

    w = [[weight(k, d) for d in range(2)] for k in range(NX)]
    for at, q in enumerate(quarters):
        rows = pl.ds(at * QUARTER, QUARTER)
        for d in range(2):
            cols = pl.ds(d * SLOT, SLOT)
            put(rows, cols, own[pl.ds(q * QUARTER, QUARTER), cols], w[0][d])
        r = lax.rem(y + NY - q, NY)
        for k in range(1, NX):
            start = pl.multiple_of(r * BUNDLE + (k - 1) * PIECE, NOTE)
            for ref, doc in ((mine, core), (other, 1 - core)):
                cols = pl.ds(pl.multiple_of((2 * k + doc) * SLOT, SLOT), SLOT)
                put(rows, cols, ref[pl.ds(start, QUARTER), :], jnp.where(doc == 0, w[k][0], w[k][1]))


def scale_kernel(clip_norm, factor, own, mine, other, hi_ref, lo_ref, ratio_ref):
    row = lax.broadcasted_iota(jnp.int32, ratio_ref.shape, 0)
    r0, r1 = (ratio_of(clip_norm, mine, other, 0, d) for d in range(2))
    ratio_ref[...] = jnp.where(row == 0, r0, r1)
    weighted(clip_norm, factor, own, mine, other, range(NY), hi_ref, lo_ref)


def step_of(mant, expo):
    return mant * jnp.exp2(expo) * (1.0 / (MANT * LIMIT))


def decode(code_ref):
    groups = code_ref.shape[0] // LANES
    tail = code_ref[pl.ds(groups * LANES, EXTRA), :].astype(jnp.int32).astype(jnp.float32)
    out = []
    for n in range(groups):
        step = step_of(tail[2 * n : 2 * n + 1], tail[2 * n + 1 : 2 * n + 2])
        out.append(code_ref[pl.ds(n * LANES, LANES), :].astype(jnp.int32).astype(jnp.float32) * step)
    return jnp.concatenate(out, axis=1)


def encode(total, out_ref):
    groups = total.shape[1] // GROUP
    row = lax.broadcasted_iota(jnp.int32, (EXTRA, GROUP), 0)
    tail = jnp.zeros((EXTRA, GROUP), jnp.float32)
    for n in range(groups):
        part = total[:, n * GROUP : (n + 1) * GROUP]
        peak = jnp.max(jnp.abs(part), axis=0, keepdims=True)
        expo = jnp.clip(jnp.floor(jnp.log2(jnp.maximum(peak, 1e-30))), -90.0, 90.0)
        mant = jnp.ceil(peak * jnp.exp2(-expo) * MANT)
        inverse = jnp.where(mant > 0.0, 1.0 / jnp.maximum(step_of(mant, expo), 1e-37), 0.0)
        q = jnp.clip(jnp.round(part * inverse), -LIMIT, LIMIT)
        out_ref[pl.ds(n * LANES, LANES), :] = q.astype(jnp.int32).astype(jnp.int16)
        tail = jnp.where(row == 2 * n, mant, jnp.where(row == 2 * n + 1, expo, tail))
    out_ref[pl.ds(groups * LANES, EXTRA), :] = tail.astype(jnp.int32).astype(jnp.int16)


def product(rows, hi_ref, lo_ref, h_refs, cols=slice(None)):
    total, token = None, 0
    for h in h_refs:
        size = h.shape[0]
        for g in (hi_ref, lo_ref):
            term = jnp.dot(g[rows, pl.ds(token, size)], h[:, cols], preferred_element_type=jnp.float32)
            total = term if total is None else total + term
        token += size
    return total


def encode_pair(low, up_j, down_j, hi_ref, lo_ref, rows, h_refs, code_refs):
    both = product(rows, hi_ref, lo_ref, h_refs)
    at = 0
    for n, out_ref in enumerate(code_refs):
        j = (up_j, down_j)[n % 2]
        width = out_ref.shape[0] // LANES * GROUP
        encode(both[(j - low) * LANES : (j - low + 1) * LANES, at : at + width], out_ref)
        at += width * (n % 2)


def opening_kernel(clip_norm, factor, own, mine, other, *refs):
    *refs, hi_ref, lo_ref = refs
    weighted(clip_norm, factor, own, mine, other, (1,), hi_ref, lo_ref)
    encode_pair(2, 3, 2, hi_ref, lo_ref, slice(None), refs[:5], refs[5:])


def first_kernel(up_j, down_j, hi_ref, lo_ref, *refs):
    low = min(up_j, down_j)
    encode_pair(low, up_j, down_j, hi_ref, lo_ref, pl.ds(low * LANES, 2 * LANES), refs[:5], refs[5:])


def later_kernel(ranges, hi_ref, lo_ref, *refs):
    *h_refs, out_ref = refs

    @pl.loop(0, out_ref.shape[1] // GROUP)
    def _(n):
        cols = pl.ds(pl.multiple_of(n * GROUP, GROUP), GROUP)
        at = 0
        for first, stop in ranges:
            size = (stop - first) * LANES
            rows = pl.ds(first * LANES, size)
            out_ref[pl.ds(at, size), cols] = product(rows, hi_ref, lo_ref, h_refs, cols)
            at += size


def hop_kernel(i, at, recv_ref, parts_ref, out_ref):
    got = decode(recv_ref)
    encode(parts_ref[pl.ds(i * LANES, LANES), pl.ds(at, got.shape[1])] + got, out_ref)


def last_kernel(i, at, first, up_ref, down_ref, parts_ref, *refs):
    out_hbm, total_ref, sem = refs[-3:]
    part = parts_ref[pl.ds(i * LANES, LANES), pl.ds(at, total_ref.shape[1])]
    total_ref[...] = part + decode(up_ref) + decode(down_ref)
    store = pltpu.make_async_copy(total_ref, out_hbm.at[:, pl.ds(first, total_ref.shape[1])], sem)
    store.start()
    store.wait()


def last(i, at, first, width, full, up, down, parts, before):
    args = tuple(map(near, (up, down, parts)))
    aliases = {}
    if before is not None:
        args += (before,)
        aliases = {3: 0}
    return pl.pallas_call(
        functools.partial(last_kernel, i, at, first),
        out_shape=jax.ShapeDtypeStruct((LANES, full), jnp.float32),
        in_specs=[VMEM] * 3 + [HBM] * (len(args) - 3),
        out_specs=HBM,
        scratch_shapes=[pltpu.VMEM((LANES, width), jnp.float32), pltpu.SemaphoreType.DMA(())],
        input_output_aliases=aliases,
        compiler_params=pltpu.CompilerParams(vmem_limit_bytes=GRANT),
        cost_estimate=cost(10**6, 10**6),
    )(*args)


def call(kernel, out_shape, flops, *args, scratch=()):
    many = isinstance(out_shape, tuple)
    return pl.pallas_call(
        kernel,
        out_shape=out_shape,
        in_specs=[VMEM] * len(args),
        out_specs=(VMEM,) * len(out_shape) if many else VMEM,
        scratch_shapes=scratch,
        compiler_params=pltpu.CompilerParams(vmem_limit_bytes=GRANT),
        cost_estimate=cost(flops, 10**6),
    )(*map(near, args))


def shift(value, axis, size, by):
    return lax.ppermute(value, axis, [(i, (i + by) % size) for i in range(size)])


def per_device(hidden, grads, lengths):
    tokens = hidden.shape[0]
    doc_total = lengths.shape[0] * NX * NZ
    ff = hidden.shape[1] * NY * 2
    model_dim = grads.shape[1]
    gathered, ready, at = [], None, 0
    for _, _, units in HALVES:
        own = lax.slice_in_dim(hidden, at, at + sum(units) * LANES, axis=1)
        at += sum(units) * LANES
        if ready is not None:
            own, ready = lax.optimization_barrier((own, ready))
        below = shift(own, "x", NX, 1)
        above = shift(own, "x", NX, -1)
        below, above = lax.optimization_barrier((below, above))
        ready = below
        far0 = shift(below[: tokens // 2], "x", NX, 1)
        far1 = shift(above[tokens // 2 :], "x", NX, -1)
        gathered.append((own, below, far0, far1, above))

    masked, *sends, note = prepare(lengths, hidden, grads)
    got = [shift(s, "x", NX, k) for k, s in enumerate(sends, 1)]
    bundle = jnp.concatenate(got + [note], axis=0)
    copies = [shift(bundle, "y", NY, r) for r in (1, 2, 3)]
    mine = jnp.concatenate([bundle] + copies, axis=0)
    other = shift(mine, "core", 2, 1)
    own = call(turn_kernel, pltpu.VMEM((NZ * LANES, tokens), grads.dtype), 10**8, masked)
    clip_norm = CLIP_RATIO * math.sqrt(SLOT * ff * model_dim)
    factor = CLIP_RATIO * math.sqrt(SLOT * doc_total)
    packs = (own, mine, other)
    wide = pltpu.VMEM((own.shape[0], NX * tokens), own.dtype)
    narrow = pltpu.VMEM((QUARTER, NX * tokens), own.dtype)
    grad_weight, first, hi, lo = None, 0, None, None
    for half, ((up_hops, down_hops, units), h) in enumerate(zip(HALVES, gathered)):
        ways = ((1, list(range(7 - up_hops, 7))), (-1, list(range(down_hops - 1, -1, -1))))
        up_j, down_j = ways[0][1][0], ways[1][1][0]
        widths = [u * LANES for u in units]
        shapes = [pltpu.VMEM((w // GROUP * LANES + EXTRA, GROUP), jnp.int16) for w in widths]
        pairs = tuple(c for c in shapes for _ in range(2))
        if half == 0:
            kernel = functools.partial(opening_kernel, clip_norm, factor)
            codes = call(kernel, pairs, 10**9, *packs, *h, scratch=[narrow, narrow])
        else:
            codes = call(functools.partial(first_kernel, up_j, down_j), pairs, 10**9, hi, lo, *h)
        codes = list(codes)
        if half == 0:
            kernel = functools.partial(scale_kernel, clip_norm, factor)
            tile = jax.ShapeDtypeStruct((8, LANES), jnp.float32)
            hi, lo, ratio = call(kernel, (wide, wide, tile), 4 * 10**6, *packs)
        parts, home = [], {}
        for n, ranges in enumerate(LATER[half]):
            order = [j for start, stop in ranges for j in range(start, stop)]
            home.update({j: (n, i) for i, j in enumerate(order)})
            shape = pltpu.VMEM((len(order) * LANES, sum(widths)), jnp.float32)
            parts.append(call(functools.partial(later_kernel, ranges), shape, 10**9, hi, lo, *h))
        for n in range(max(up_hops, down_hops)):
            for stream, code in enumerate(shapes):
                for side, (way, order) in enumerate(ways):
                    if n < len(order):
                        at = 2 * stream + side
                        if n:
                            p, i = home[order[n]]
                            kernel = functools.partial(hop_kernel, i, sum(widths[:stream]))
                            codes[at] = call(kernel, code, 10**6, codes[at], parts[p])
                        codes[at] = shift(codes[at], "z", NZ, way)
        p, i = home[NZ - 1]
        for stream, width in enumerate(widths):
            at = sum(widths[:stream])
            pair = codes[2 * stream : 2 * stream + 2]
            grad_weight = last(i, at, first + at, width, hidden.shape[1], *pair, parts[p], grad_weight)
        first += sum(widths)
    return grad_weight, ratio[:2, 0]


def solution(mesh):
    fine = Mesh(mesh.devices.reshape(NZ, NX, NY, 2), ("z", "x", "y", "core"))
    doc, tensor = ("z", "x"), ("y", "core")
    return jax.shard_map(
        per_device,
        mesh=fine,
        in_specs=(P(doc, tensor), P(doc, None), P(doc)),
        out_specs=(P(doc, tensor), P(doc)),
        check_vma=False,
    )
```

```python
import functools
import math

import jax
import jax.numpy as jnp
from jax import lax
from jax.experimental import pallas as pl
from jax.experimental.pallas import tpu as pltpu
from jax.sharding import Mesh, PartitionSpec as P

SLOT = 128
CLIP_RATIO = 2.0
EPSILON = 1e-06
NX, NY, NZ = 4, 4, 8
LANES = 128
QUARTER = NZ * LANES // NY
NOTE = 16
PIECE = QUARTER + NOTE
BUNDLE = (NX - 1) * PIECE + NOTE
HALVES = ((4, 3, 6), (3, 4, 8))
LATER = ((((0, 2), (4, 6)), ((6, 8),)), (((1, 3), (5, 7)), ((0, 1), (7, 8))))
LIMIT = 32767.0
MANT = 8192.0
EXTRA = 8
GROUP = 256
GRANT = 24 * 2**20

SMEM = pl.BlockSpec(memory_space=pltpu.SMEM)
VMEM = pl.BlockSpec(memory_space=pltpu.VMEM)
HBM = pl.BlockSpec(memory_space=pltpu.HBM)
NT = (((1,), (1,)), ((), ()))


def cost(flops, nbytes):
    return pl.CostEstimate(flops=flops, bytes_accessed=nbytes, transcendentals=0)


def near(value):
    return pltpu.with_memory_space_constraint(value, pltpu.VMEM)


def split(value):
    hi = value.astype(jnp.bfloat16)
    rest = value - hi.astype(jnp.float32)
    mid = rest.astype(jnp.bfloat16)
    return hi, mid, (rest - mid.astype(jnp.float32)).astype(jnp.bfloat16)


def turned(masked_ref, rows, j, dest):
    r = lax.broadcasted_iota(jnp.int32, (LANES, LANES), 0)
    c = lax.broadcasted_iota(jnp.int32, (LANES, LANES), 1)
    eye = jnp.where(r == c, 1.0, 0.0).astype(masked_ref.dtype)
    block = lax.rem(lax.axis_index("z") + 2 * NZ - 1 - j, NZ) * NX + dest
    piece = masked_ref[rows, pl.ds(pl.multiple_of(block * LANES, LANES), LANES)]
    return lax.dot_general(eye, piece, NT, preferred_element_type=jnp.float32).astype(piece.dtype)


def turn_kernel(masked_ref, own_ref):
    x = lax.axis_index("x")
    for j in range(NZ):
        own_ref[pl.ds(j * LANES, LANES), :] = turned(masked_ref, slice(None), j, x)


def prepare_kernel(len_hbm, hidden_hbm, grads_hbm, masked_ref, s1, s2, s3, note_ref, grads_ref, hidden_ref, len_ref, sem, len_sem):
    lengths = pltpu.make_async_copy(len_hbm, len_ref, len_sem)
    lengths.start()
    loads = [
        pltpu.make_async_copy(src.at[pl.ds(d * SLOT, SLOT), :], dst.at[pl.ds(d * SLOT, SLOT), :], sem.at[i, d])
        for d in range(2)
        for i, (src, dst) in enumerate(((grads_hbm, grads_ref), (hidden_hbm, hidden_ref)))
    ]
    for load in loads:
        load.start()
    x, y, core = (lax.axis_index(a) for a in ("x", "y", "core"))
    row = lax.broadcasted_iota(jnp.int32, note_ref.shape, 0)
    note = jnp.zeros(note_ref.shape, jnp.float32)
    for d in range(2):
        rows = pl.ds(d * SLOT, SLOT)
        if d == 0:
            lengths.wait()
        loads[2 * d].wait()
        g = grads_ref[rows, :]
        token = lax.broadcasted_iota(jnp.int32, g.shape, 0)
        m = jnp.where(token < len_ref[d], g.astype(jnp.float32), 0.0).astype(g.dtype)
        masked_ref[rows, :] = m
        loads[2 * d + 1].wait()
        h = hidden_ref[rows, :]
        gram_g = lax.dot_general(m, m, NT, preferred_element_type=jnp.float32)
        gram_h = lax.dot_general(h, h, NT, preferred_element_type=jnp.float32)
        square = jnp.sum(gram_g * gram_h)
        whole = jnp.zeros(note_ref.shape, jnp.float32) + square
        for i, term in enumerate(split(whole)):
            note = jnp.where(row == 3 * d + i, term.astype(jnp.float32), note)
    note = note.astype(note_ref.dtype)
    note_ref[...] = note

    mine = pl.ds(pl.multiple_of(core * SLOT, SLOT), SLOT)
    for k, send in enumerate((s1, s2, s3), 1):
        dest = lax.rem(x + k, NX)
        for i in range(QUARTER // LANES):
            send[pl.ds(i * LANES, LANES), :] = turned(masked_ref, mine, y * (QUARTER // LANES) + i, dest)
        send[pl.ds(QUARTER, NOTE), :] = note


def prepare(lengths, hidden, grads):
    piece = pltpu.VMEM((PIECE, LANES), grads.dtype)
    return pl.pallas_call(
        prepare_kernel,
        out_shape=(
            pltpu.VMEM(grads.shape, grads.dtype),
            piece,
            piece,
            piece,
            pltpu.VMEM((NOTE, LANES), grads.dtype),
        ),
        in_specs=[HBM, HBM, HBM],
        out_specs=(VMEM,) * 5,
        scratch_shapes=[
            pltpu.VMEM(grads.shape, grads.dtype),
            pltpu.VMEM(hidden.shape, hidden.dtype),
            pltpu.SMEM(lengths.shape, lengths.dtype),
            pltpu.SemaphoreType.DMA((2, 2)),
            pltpu.SemaphoreType.DMA(()),
        ],
        compiler_params=pltpu.CompilerParams(vmem_limit_bytes=GRANT),
        cost_estimate=cost(4 * 10**8, 5 * 10**6),
    )(
        pltpu.with_memory_space_constraint(lengths, pltpu.HBM),
        pltpu.with_memory_space_constraint(hidden, pltpu.HBM),
        pltpu.with_memory_space_constraint(grads, pltpu.HBM),
    )


def ratio_of(clip_norm, mine, other, k, d):
    start = (NX - 1) * PIECE if k == 0 else (k - 1) * PIECE + QUARTER

    def partial(ref, r):
        note = ref[pl.ds(r * BUNDLE + start, NOTE), :].astype(jnp.float32)
        return note[3 * d : 3 * d + 1] + note[3 * d + 1 : 3 * d + 2] + note[3 * d + 2 : 3 * d + 3]

    def of(ref):
        return (partial(ref, 0) + partial(ref, 2)) + (partial(ref, 1) + partial(ref, 3))

    return jnp.sqrt(of(mine) + of(other) + EPSILON) / clip_norm


def weighted(clip_norm, factor, own, mine, other, quarters, hi_ref, lo_ref):
    y, core = lax.axis_index("y"), lax.axis_index("core")

    def put(rows, cols, value, w):
        scaled = value.astype(jnp.float32) * w
        hi = scaled.astype(hi_ref.dtype)
        hi_ref[rows, cols] = hi
        lo_ref[rows, cols] = (scaled - hi.astype(jnp.float32)).astype(lo_ref.dtype)

    def weight(k, d):
        return jnp.minimum(1.0, 1.0 / ratio_of(clip_norm, mine, other, k, d)) / factor

    w = [[weight(k, d) for d in range(2)] for k in range(NX)]
    for at, q in enumerate(quarters):
        rows = pl.ds(at * QUARTER, QUARTER)
        for d in range(2):
            cols = pl.ds(d * SLOT, SLOT)
            put(rows, cols, own[pl.ds(q * QUARTER, QUARTER), cols], w[0][d])
        r = lax.rem(y + NY - q, NY)
        for k in range(1, NX):
            start = pl.multiple_of(r * BUNDLE + (k - 1) * PIECE, NOTE)
            for ref, doc in ((mine, core), (other, 1 - core)):
                cols = pl.ds(pl.multiple_of((2 * k + doc) * SLOT, SLOT), SLOT)
                put(rows, cols, ref[pl.ds(start, QUARTER), :], jnp.where(doc == 0, w[k][0], w[k][1]))


def scale_kernel(clip_norm, factor, own, mine, other, hi_ref, lo_ref, ratio_ref):
    row = lax.broadcasted_iota(jnp.int32, ratio_ref.shape, 0)
    r0, r1 = (ratio_of(clip_norm, mine, other, 0, d) for d in range(2))
    ratio_ref[...] = jnp.where(row == 0, r0, r1)
    weighted(clip_norm, factor, own, mine, other, range(NY), hi_ref, lo_ref)


def step_of(mant, expo):
    return mant * jnp.exp2(expo) * (1.0 / (MANT * LIMIT))


def decode(code_ref):
    groups = code_ref.shape[0] // LANES
    tail = code_ref[pl.ds(groups * LANES, EXTRA), :].astype(jnp.int32).astype(jnp.float32)
    out = []
    for n in range(groups):
        step = step_of(tail[2 * n : 2 * n + 1], tail[2 * n + 1 : 2 * n + 2])
        out.append(code_ref[pl.ds(n * LANES, LANES), :].astype(jnp.int32).astype(jnp.float32) * step)
    return jnp.concatenate(out, axis=1)


def encode(total, out_ref):
    groups = total.shape[1] // GROUP
    row = lax.broadcasted_iota(jnp.int32, (EXTRA, GROUP), 0)
    tail = jnp.zeros((EXTRA, GROUP), jnp.float32)
    for n in range(groups):
        part = total[:, n * GROUP : (n + 1) * GROUP]
        peak = jnp.max(jnp.abs(part), axis=0, keepdims=True)
        expo = jnp.clip(jnp.floor(jnp.log2(jnp.maximum(peak, 1e-30))), -90.0, 90.0)
        mant = jnp.ceil(peak * jnp.exp2(-expo) * MANT)
        inverse = jnp.where(mant > 0.0, 1.0 / jnp.maximum(step_of(mant, expo), 1e-37), 0.0)
        q = jnp.clip(jnp.round(part * inverse), -LIMIT, LIMIT)
        out_ref[pl.ds(n * LANES, LANES), :] = q.astype(jnp.int32).astype(jnp.int16)
        tail = jnp.where(row == 2 * n, mant, jnp.where(row == 2 * n + 1, expo, tail))
    out_ref[pl.ds(groups * LANES, EXTRA), :] = tail.astype(jnp.int32).astype(jnp.int16)


def product(rows, hi_ref, lo_ref, h_refs):
    total, token = None, 0
    for h in h_refs:
        size = h.shape[0]
        for g in (hi_ref, lo_ref):
            term = jnp.dot(g[rows, pl.ds(token, size)], h[...], preferred_element_type=jnp.float32)
            total = term if total is None else total + term
        token += size
    return total


def encode_pair(low, up_j, down_j, hi_ref, lo_ref, rows, h_refs, up_ref, down_ref):
    both = product(rows, hi_ref, lo_ref, h_refs)
    for j, out_ref in ((up_j, up_ref), (down_j, down_ref)):
        encode(both[(j - low) * LANES : (j - low + 1) * LANES], out_ref)


def opening_kernel(clip_norm, factor, own, mine, other, *refs):
    *h_refs, up_ref, down_ref, hi_ref, lo_ref = refs
    weighted(clip_norm, factor, own, mine, other, (1,), hi_ref, lo_ref)
    encode_pair(2, 3, 2, hi_ref, lo_ref, slice(None), h_refs, up_ref, down_ref)


def first_kernel(up_j, down_j, hi_ref, lo_ref, *refs):
    *h_refs, up_ref, down_ref = refs
    low = min(up_j, down_j)
    encode_pair(low, up_j, down_j, hi_ref, lo_ref, pl.ds(low * LANES, 2 * LANES), h_refs, up_ref, down_ref)


def later_kernel(ranges, hi_ref, lo_ref, *refs):
    *h_refs, out_ref = refs
    at = 0
    for first, stop in ranges:
        size = (stop - first) * LANES
        out_ref[pl.ds(at, size), :] = product(pl.ds(first * LANES, size), hi_ref, lo_ref, h_refs)
        at += size


def hop_kernel(i, recv_ref, parts_ref, out_ref):
    total = parts_ref[pl.ds(i * LANES, LANES), :] + decode(recv_ref)
    encode(total, out_ref)


def last_kernel(i, first, up_ref, down_ref, parts_ref, *refs):
    out_hbm, total_ref, sem = refs[-3:]
    total_ref[...] = parts_ref[pl.ds(i * LANES, LANES), :] + decode(up_ref) + decode(down_ref)
    store = pltpu.make_async_copy(total_ref, out_hbm.at[:, pl.ds(first, total_ref.shape[1])], sem)
    store.start()
    store.wait()


def last(i, first, full, up, down, parts, before):
    width = parts.shape[1]
    args = tuple(map(near, (up, down, parts)))
    aliases = {}
    if before is not None:
        args += (before,)
        aliases = {3: 0}
    return pl.pallas_call(
        functools.partial(last_kernel, i, first),
        out_shape=jax.ShapeDtypeStruct((LANES, full), jnp.float32),
        in_specs=[VMEM] * 3 + [HBM] * (len(args) - 3),
        out_specs=HBM,
        scratch_shapes=[pltpu.VMEM((LANES, width), jnp.float32), pltpu.SemaphoreType.DMA(())],
        input_output_aliases=aliases,
        compiler_params=pltpu.CompilerParams(vmem_limit_bytes=GRANT),
        cost_estimate=cost(10**6, 10**6),
    )(*args)


def call(kernel, out_shape, flops, *args, scratch=()):
    many = isinstance(out_shape, tuple)
    return pl.pallas_call(
        kernel,
        out_shape=out_shape,
        in_specs=[VMEM] * len(args),
        out_specs=(VMEM,) * len(out_shape) if many else VMEM,
        scratch_shapes=scratch,
        compiler_params=pltpu.CompilerParams(vmem_limit_bytes=GRANT),
        cost_estimate=cost(flops, 10**6),
    )(*map(near, args))


def shift(value, axis, size, by):
    return lax.ppermute(value, axis, [(i, (i + by) % size) for i in range(size)])


def per_device(hidden, grads, lengths):
    tokens = hidden.shape[0]
    doc_total = lengths.shape[0] * NX * NZ
    ff = hidden.shape[1] * NY * 2
    model_dim = grads.shape[1]
    gathered, at = [], 0
    for n, (_, _, units) in enumerate(HALVES):
        own = lax.slice_in_dim(hidden, at, at + units * LANES, axis=1)
        at += units * LANES
        below = shift(own, "x", NX, 1)
        above = shift(own, "x", NX, -1)
        if n == 0:
            far = (shift(own, "x", NX, 2),)
        if n:
            below, above = lax.optimization_barrier((below, above))
            half = tokens // 2
            far = (shift(below[:half], "x", NX, 1), shift(above[half:], "x", NX, -1))
        gathered.append((own, below, *far, above))

    masked, *sends, note = prepare(lengths, hidden, grads)
    got = [shift(s, "x", NX, k) for k, s in enumerate(sends, 1)]
    bundle = jnp.concatenate(got + [note], axis=0)
    copies = [shift(bundle, "y", NY, r) for r in (1, 2, 3)]
    mine = jnp.concatenate([bundle] + copies, axis=0)
    other = shift(mine, "core", 2, 1)
    own = call(turn_kernel, pltpu.VMEM((NZ * LANES, tokens), grads.dtype), 10**8, masked)
    clip_norm = CLIP_RATIO * math.sqrt(SLOT * ff * model_dim)
    factor = CLIP_RATIO * math.sqrt(SLOT * doc_total)
    packs = (own, mine, other)
    wide = pltpu.VMEM((own.shape[0], NX * tokens), own.dtype)
    narrow = pltpu.VMEM((QUARTER, NX * tokens), own.dtype)
    grad_weight, first, hi, lo = None, 0, None, None
    for half, ((up_hops, down_hops, units), h) in enumerate(zip(HALVES, gathered)):
        up, down = list(range(7 - up_hops, 7)), list(range(down_hops - 1, -1, -1))
        width = units * LANES
        code = pltpu.VMEM((width // GROUP * LANES + EXTRA, GROUP), jnp.int16)
        if half == 0:
            kernel = functools.partial(opening_kernel, clip_norm, factor)
            codes = call(kernel, (code, code), 10**9, *packs, *h, scratch=[narrow, narrow])
        else:
            kernel = functools.partial(first_kernel, up[0], down[0])
            codes = call(kernel, (code, code), 10**9, hi, lo, *h)
        codes = list(codes)
        if half == 0:
            kernel = functools.partial(scale_kernel, clip_norm, factor)
            tile = jax.ShapeDtypeStruct((8, LANES), jnp.float32)
            hi, lo, ratio = call(kernel, (wide, wide, tile), 4 * 10**6, *packs)
        parts, home = [], {}
        for n, ranges in enumerate(LATER[half]):
            order = [j for start, stop in ranges for j in range(start, stop)]
            home.update({j: (n, i) for i, j in enumerate(order)})
            shape = pltpu.VMEM((len(order) * LANES, width), jnp.float32)
            parts.append(call(functools.partial(later_kernel, ranges), shape, 10**9, hi, lo, *h))
        for n in range(max(up_hops, down_hops)):
            for at, (way, order) in enumerate(((1, up), (-1, down))):
                if n < len(order):
                    if n:
                        p, i = home[order[n]]
                        kernel = functools.partial(hop_kernel, i)
                        codes[at] = call(kernel, code, 10**6, codes[at], parts[p])
                    codes[at] = shift(codes[at], "z", NZ, way)
        p, i = home[NZ - 1]
        grad_weight = last(i, first, hidden.shape[1], *codes, parts[p], grad_weight)
        first += width
    return grad_weight, ratio[:2, 0]


def solution(mesh):
    fine = Mesh(mesh.devices.reshape(NZ, NX, NY, 2), ("z", "x", "y", "core"))
    doc, tensor = ("z", "x"), ("y", "core")
    return jax.shard_map(
        per_device,
        mesh=fine,
        in_specs=(P(doc, tensor), P(doc, None), P(doc)),
        out_specs=(P(doc, tensor), P(doc)),
        check_vma=False,
    )
```

```python
import functools
import math

import jax
import jax.numpy as jnp
from jax import lax
from jax.experimental import pallas as pl
from jax.experimental.pallas import tpu as pltpu
from jax.sharding import Mesh, PartitionSpec as P

SLOT = 128
CLIP_RATIO = 2.0
EPSILON = 1e-06
NX, NY, NZ = 4, 4, 8
LANES = 128
QUARTER = NZ * LANES // NY
NOTE = 16
PIECE = QUARTER + NOTE
BUNDLE = (NX - 1) * PIECE + NOTE
HALVES = ((4, 3, 6), (3, 4, 8))
LATER = ((((0, 2), (4, 6)), ((6, 8),)), (((1, 3), (5, 7)), ((0, 1), (7, 8))))
LIMIT = 32767.0
MANT = 8192.0
EXTRA = 8
GROUP = 256
GRANT = 24 * 2**20

SMEM = pl.BlockSpec(memory_space=pltpu.SMEM)
VMEM = pl.BlockSpec(memory_space=pltpu.VMEM)
HBM = pl.BlockSpec(memory_space=pltpu.HBM)
NT = (((1,), (1,)), ((), ()))


def cost(flops, nbytes):
    return pl.CostEstimate(flops=flops, bytes_accessed=nbytes, transcendentals=0)


def near(value):
    return pltpu.with_memory_space_constraint(value, pltpu.VMEM)


def split(value):
    hi = value.astype(jnp.bfloat16)
    rest = value - hi.astype(jnp.float32)
    mid = rest.astype(jnp.bfloat16)
    return hi, mid, (rest - mid.astype(jnp.float32)).astype(jnp.bfloat16)


def turned(masked_ref, rows, j, dest):
    r = lax.broadcasted_iota(jnp.int32, (LANES, LANES), 0)
    c = lax.broadcasted_iota(jnp.int32, (LANES, LANES), 1)
    eye = jnp.where(r == c, 1.0, 0.0).astype(masked_ref.dtype)
    block = lax.rem(lax.axis_index("z") + 2 * NZ - 1 - j, NZ) * NX + dest
    piece = masked_ref[rows, pl.ds(pl.multiple_of(block * LANES, LANES), LANES)]
    return lax.dot_general(eye, piece, NT, preferred_element_type=jnp.float32).astype(piece.dtype)


def turn_kernel(masked_ref, own_ref):
    x = lax.axis_index("x")
    for j in range(NZ):
        own_ref[pl.ds(j * LANES, LANES), :] = turned(masked_ref, slice(None), j, x)


def prepare_kernel(len_hbm, hidden_hbm, grads_hbm, masked_ref, s1, s2, s3, note_ref, grads_ref, hidden_ref, len_ref, sem, len_sem):
    lengths = pltpu.make_async_copy(len_hbm, len_ref, len_sem)
    lengths.start()
    piece = SLOT // 4

    def copies(i, d):
        src, dst = ((grads_hbm, grads_ref), (hidden_hbm, hidden_ref))[i]
        rows = [pl.ds(d * SLOT + n * piece, piece) for n in range(4)]
        return [pltpu.make_async_copy(src.at[r, :], dst.at[r, :], sem.at[i, d, n]) for n, r in enumerate(rows)]

    groups = [copies(i, d) for d in range(2) for i in range(2)]
    loads = [c for g in groups for c in g]
    for load in loads:
        load.start()
    x, y, core = (lax.axis_index(a) for a in ("x", "y", "core"))
    row = lax.broadcasted_iota(jnp.int32, note_ref.shape, 0)
    note = jnp.zeros(note_ref.shape, jnp.float32)
    for d in range(2):
        rows = pl.ds(d * SLOT, SLOT)
        if d == 0:
            lengths.wait()
        for load in groups[2 * d]:
            load.wait()
        g = grads_ref[rows, :]
        token = lax.broadcasted_iota(jnp.int32, g.shape, 0)
        m = jnp.where(token < len_ref[d], g.astype(jnp.float32), 0.0).astype(g.dtype)
        masked_ref[rows, :] = m
        for load in groups[2 * d + 1]:
            load.wait()
        h = hidden_ref[rows, :]
        gram_g = lax.dot_general(m, m, NT, preferred_element_type=jnp.float32)
        gram_h = lax.dot_general(h, h, NT, preferred_element_type=jnp.float32)
        square = jnp.sum(gram_g * gram_h)
        whole = jnp.zeros(note_ref.shape, jnp.float32) + square
        for i, term in enumerate(split(whole)):
            note = jnp.where(row == 3 * d + i, term.astype(jnp.float32), note)
    note = note.astype(note_ref.dtype)
    note_ref[...] = note

    mine = pl.ds(pl.multiple_of(core * SLOT, SLOT), SLOT)
    for k, send in enumerate((s1, s2, s3), 1):
        dest = lax.rem(x + k, NX)
        for i in range(QUARTER // LANES):
            send[pl.ds(i * LANES, LANES), :] = turned(masked_ref, mine, y * (QUARTER // LANES) + i, dest)
        send[pl.ds(QUARTER, NOTE), :] = note


def prepare(lengths, hidden, grads):
    piece = pltpu.VMEM((PIECE, LANES), grads.dtype)
    return pl.pallas_call(
        prepare_kernel,
        out_shape=(
            pltpu.VMEM(grads.shape, grads.dtype),
            piece,
            piece,
            piece,
            pltpu.VMEM((NOTE, LANES), grads.dtype),
        ),
        in_specs=[HBM, HBM, HBM],
        out_specs=(VMEM,) * 5,
        scratch_shapes=[
            pltpu.VMEM(grads.shape, grads.dtype),
            pltpu.VMEM(hidden.shape, hidden.dtype),
            pltpu.SMEM(lengths.shape, lengths.dtype),
            pltpu.SemaphoreType.DMA((2, 2, 4)),
            pltpu.SemaphoreType.DMA(()),
        ],
        compiler_params=pltpu.CompilerParams(vmem_limit_bytes=GRANT),
        cost_estimate=cost(4 * 10**8, 5 * 10**6),
    )(
        pltpu.with_memory_space_constraint(lengths, pltpu.HBM),
        pltpu.with_memory_space_constraint(hidden, pltpu.HBM),
        pltpu.with_memory_space_constraint(grads, pltpu.HBM),
    )


def ratio_of(clip_norm, mine, other, k, d):
    start = (NX - 1) * PIECE if k == 0 else (k - 1) * PIECE + QUARTER

    def partial(ref, r):
        note = ref[pl.ds(r * BUNDLE + start, NOTE), :].astype(jnp.float32)
        return note[3 * d : 3 * d + 1] + note[3 * d + 1 : 3 * d + 2] + note[3 * d + 2 : 3 * d + 3]

    def of(ref):
        return (partial(ref, 0) + partial(ref, 2)) + (partial(ref, 1) + partial(ref, 3))

    return jnp.sqrt(of(mine) + of(other) + EPSILON) / clip_norm


def weighted(clip_norm, factor, own, mine, other, quarters, hi_ref, lo_ref):
    y, core = lax.axis_index("y"), lax.axis_index("core")

    def put(rows, cols, value, w):
        scaled = value.astype(jnp.float32) * w
        hi = scaled.astype(hi_ref.dtype)
        hi_ref[rows, cols] = hi
        lo_ref[rows, cols] = (scaled - hi.astype(jnp.float32)).astype(lo_ref.dtype)

    def weight(k, d):
        return jnp.minimum(1.0, 1.0 / ratio_of(clip_norm, mine, other, k, d)) / factor

    w = [[weight(k, d) for d in range(2)] for k in range(NX)]
    for at, q in enumerate(quarters):
        rows = pl.ds(at * QUARTER, QUARTER)
        for d in range(2):
            cols = pl.ds(d * SLOT, SLOT)
            put(rows, cols, own[pl.ds(q * QUARTER, QUARTER), cols], w[0][d])
        r = lax.rem(y + NY - q, NY)
        for k in range(1, NX):
            start = pl.multiple_of(r * BUNDLE + (k - 1) * PIECE, NOTE)
            for ref, doc in ((mine, core), (other, 1 - core)):
                cols = pl.ds(pl.multiple_of((2 * k + doc) * SLOT, SLOT), SLOT)
                put(rows, cols, ref[pl.ds(start, QUARTER), :], jnp.where(doc == 0, w[k][0], w[k][1]))


def scale_kernel(clip_norm, factor, own, mine, other, hi_ref, lo_ref, ratio_ref):
    row = lax.broadcasted_iota(jnp.int32, ratio_ref.shape, 0)
    r0, r1 = (ratio_of(clip_norm, mine, other, 0, d) for d in range(2))
    ratio_ref[...] = jnp.where(row == 0, r0, r1)
    weighted(clip_norm, factor, own, mine, other, range(NY), hi_ref, lo_ref)


def step_of(mant, expo):
    return mant * jnp.exp2(expo) * (1.0 / (MANT * LIMIT))


def decode(code_ref):
    groups = code_ref.shape[0] // LANES
    tail = code_ref[pl.ds(groups * LANES, EXTRA), :].astype(jnp.int32).astype(jnp.float32)
    out = []
    for n in range(groups):
        step = step_of(tail[2 * n : 2 * n + 1], tail[2 * n + 1 : 2 * n + 2])
        out.append(code_ref[pl.ds(n * LANES, LANES), :].astype(jnp.int32).astype(jnp.float32) * step)
    return jnp.concatenate(out, axis=1)


def encode(total, out_ref):
    groups = total.shape[1] // GROUP
    row = lax.broadcasted_iota(jnp.int32, (EXTRA, GROUP), 0)
    tail = jnp.zeros((EXTRA, GROUP), jnp.float32)
    for n in range(groups):
        part = total[:, n * GROUP : (n + 1) * GROUP]
        peak = jnp.max(jnp.abs(part), axis=0, keepdims=True)
        expo = jnp.clip(jnp.floor(jnp.log2(jnp.maximum(peak, 1e-30))), -90.0, 90.0)
        mant = jnp.ceil(peak * jnp.exp2(-expo) * MANT)
        inverse = jnp.where(mant > 0.0, 1.0 / jnp.maximum(step_of(mant, expo), 1e-37), 0.0)
        q = jnp.clip(jnp.round(part * inverse), -LIMIT, LIMIT)
        out_ref[pl.ds(n * LANES, LANES), :] = q.astype(jnp.int32).astype(jnp.int16)
        tail = jnp.where(row == 2 * n, mant, jnp.where(row == 2 * n + 1, expo, tail))
    out_ref[pl.ds(groups * LANES, EXTRA), :] = tail.astype(jnp.int32).astype(jnp.int16)


def product(rows, hi_ref, lo_ref, h_refs):
    total, token = None, 0
    for h in h_refs:
        size = h.shape[0]
        for g in (hi_ref, lo_ref):
            term = jnp.dot(g[rows, pl.ds(token, size)], h[...], preferred_element_type=jnp.float32)
            total = term if total is None else total + term
        token += size
    return total


def encode_pair(low, up_j, down_j, hi_ref, lo_ref, rows, h_refs, up_ref, down_ref):
    both = product(rows, hi_ref, lo_ref, h_refs)
    for j, out_ref in ((up_j, up_ref), (down_j, down_ref)):
        encode(both[(j - low) * LANES : (j - low + 1) * LANES], out_ref)


def opening_kernel(clip_norm, factor, own, mine, other, *refs):
    *h_refs, up_ref, down_ref, hi_ref, lo_ref = refs
    weighted(clip_norm, factor, own, mine, other, (1,), hi_ref, lo_ref)
    encode_pair(2, 3, 2, hi_ref, lo_ref, slice(None), h_refs, up_ref, down_ref)


def first_kernel(up_j, down_j, hi_ref, lo_ref, *refs):
    *h_refs, up_ref, down_ref = refs
    low = min(up_j, down_j)
    encode_pair(low, up_j, down_j, hi_ref, lo_ref, pl.ds(low * LANES, 2 * LANES), h_refs, up_ref, down_ref)


def later_kernel(ranges, hi_ref, lo_ref, *refs):
    *h_refs, out_ref = refs
    at = 0
    for first, stop in ranges:
        size = (stop - first) * LANES
        out_ref[pl.ds(at, size), :] = product(pl.ds(first * LANES, size), hi_ref, lo_ref, h_refs)
        at += size


def hop_kernel(i, recv_ref, parts_ref, out_ref):
    total = parts_ref[pl.ds(i * LANES, LANES), :] + decode(recv_ref)
    encode(total, out_ref)


def last_kernel(i, first, up_ref, down_ref, parts_ref, *refs):
    out_hbm, total_ref, sem = refs[-3:]
    total_ref[...] = parts_ref[pl.ds(i * LANES, LANES), :] + decode(up_ref) + decode(down_ref)
    store = pltpu.make_async_copy(total_ref, out_hbm.at[:, pl.ds(first, total_ref.shape[1])], sem)
    store.start()
    store.wait()


def last(i, first, full, up, down, parts, before):
    width = parts.shape[1]
    args = tuple(map(near, (up, down, parts)))
    aliases = {}
    if before is not None:
        args += (before,)
        aliases = {3: 0}
    return pl.pallas_call(
        functools.partial(last_kernel, i, first),
        out_shape=jax.ShapeDtypeStruct((LANES, full), jnp.float32),
        in_specs=[VMEM] * 3 + [HBM] * (len(args) - 3),
        out_specs=HBM,
        scratch_shapes=[pltpu.VMEM((LANES, width), jnp.float32), pltpu.SemaphoreType.DMA(())],
        input_output_aliases=aliases,
        compiler_params=pltpu.CompilerParams(vmem_limit_bytes=GRANT),
        cost_estimate=cost(10**6, 10**6),
    )(*args)


def call(kernel, out_shape, flops, *args, scratch=()):
    many = isinstance(out_shape, tuple)
    return pl.pallas_call(
        kernel,
        out_shape=out_shape,
        in_specs=[VMEM] * len(args),
        out_specs=(VMEM,) * len(out_shape) if many else VMEM,
        scratch_shapes=scratch,
        compiler_params=pltpu.CompilerParams(vmem_limit_bytes=GRANT),
        cost_estimate=cost(flops, 10**6),
    )(*map(near, args))


def shift(value, axis, size, by):
    return lax.ppermute(value, axis, [(i, (i + by) % size) for i in range(size)])


def per_device(hidden, grads, lengths):
    tokens = hidden.shape[0]
    doc_total = lengths.shape[0] * NX * NZ
    ff = hidden.shape[1] * NY * 2
    model_dim = grads.shape[1]
    gathered, ready, at = [], None, 0
    for _, _, units in HALVES:
        own = lax.slice_in_dim(hidden, at, at + units * LANES, axis=1)
        at += units * LANES
        if ready is not None:
            own, ready = lax.optimization_barrier((own, ready))
        below = shift(own, "x", NX, 1)
        above = shift(own, "x", NX, -1)
        below, above = lax.optimization_barrier((below, above))
        ready = below
        far0 = shift(below[: tokens // 2], "x", NX, 1)
        far1 = shift(above[tokens // 2 :], "x", NX, -1)
        gathered.append((own, below, far0, far1, above))

    masked, *sends, note = prepare(lengths, hidden, grads)
    got = [shift(s, "x", NX, k) for k, s in enumerate(sends, 1)]
    bundle = jnp.concatenate(got + [note], axis=0)
    copies = [shift(bundle, "y", NY, r) for r in (1, 2, 3)]
    mine = jnp.concatenate([bundle] + copies, axis=0)
    other = shift(mine, "core", 2, 1)
    own = call(turn_kernel, pltpu.VMEM((NZ * LANES, tokens), grads.dtype), 10**8, masked)
    clip_norm = CLIP_RATIO * math.sqrt(SLOT * ff * model_dim)
    factor = CLIP_RATIO * math.sqrt(SLOT * doc_total)
    packs = (own, mine, other)
    wide = pltpu.VMEM((own.shape[0], NX * tokens), own.dtype)
    narrow = pltpu.VMEM((QUARTER, NX * tokens), own.dtype)
    grad_weight, first, hi, lo = None, 0, None, None
    for half, ((up_hops, down_hops, units), h) in enumerate(zip(HALVES, gathered)):
        up, down = list(range(7 - up_hops, 7)), list(range(down_hops - 1, -1, -1))
        width = units * LANES
        code = pltpu.VMEM((width // GROUP * LANES + EXTRA, GROUP), jnp.int16)
        if half == 0:
            kernel = functools.partial(opening_kernel, clip_norm, factor)
            codes = call(kernel, (code, code), 10**9, *packs, *h, scratch=[narrow, narrow])
        else:
            kernel = functools.partial(first_kernel, up[0], down[0])
            codes = call(kernel, (code, code), 10**9, hi, lo, *h)
        codes = list(codes)
        if half == 0:
            kernel = functools.partial(scale_kernel, clip_norm, factor)
            tile = jax.ShapeDtypeStruct((8, LANES), jnp.float32)
            hi, lo, ratio = call(kernel, (wide, wide, tile), 4 * 10**6, *packs)
        parts, home = [], {}
        for n, ranges in enumerate(LATER[half]):
            order = [j for start, stop in ranges for j in range(start, stop)]
            home.update({j: (n, i) for i, j in enumerate(order)})
            shape = pltpu.VMEM((len(order) * LANES, width), jnp.float32)
            parts.append(call(functools.partial(later_kernel, ranges), shape, 10**9, hi, lo, *h))
        for n in range(max(up_hops, down_hops)):
            for at, (way, order) in enumerate(((1, up), (-1, down))):
                if n < len(order):
                    if n:
                        p, i = home[order[n]]
                        kernel = functools.partial(hop_kernel, i)
                        codes[at] = call(kernel, code, 10**6, codes[at], parts[p])
                    codes[at] = shift(codes[at], "z", NZ, way)
        p, i = home[NZ - 1]
        grad_weight = last(i, first, hidden.shape[1], *codes, parts[p], grad_weight)
        first += width
    return grad_weight, ratio[:2, 0]


def solution(mesh):
    fine = Mesh(mesh.devices.reshape(NZ, NX, NY, 2), ("z", "x", "y", "core"))
    doc, tensor = ("z", "x"), ("y", "core")
    return jax.shard_map(
        per_device,
        mesh=fine,
        in_specs=(P(doc, tensor), P(doc, None), P(doc)),
        out_specs=(P(doc, tensor), P(doc)),
        check_vma=False,
    )
```
